1024 devices in a mesh: gx: 32 (over z_hi, y, core), gy: 4 (over x), gz: 8 (over z_lo).
Axes of the slice: x: 4, y: 4, z: 32 (z_hi: 4, z_lo: 8; z = z_hi * 8 + z_lo), core: 2. Of those that a mesh axis runs over, the one named last changes fastest.
Arguments:
- displacement: float32 [3, 64, 32, 1024], P(None, 'gx', 'gy', 'gz'), may hold values from -6 to 6
- displacement_old: float32 [3, 64, 32, 1024], P(None, 'gx', 'gy', 'gz'), may hold values from -6 to 6
- visco_state: float32 [6, 6, 64, 32, 1024], P(None, None, 'gx', 'gy', 'gz'), may hold values from -3 to 3
- energy_max: float32 [64, 32, 1024], P('gx', 'gy', 'gz'), may hold values from 0.1 to 4
- region: int32 [64, 32, 1024], P('gx', 'gy', 'gz'), may hold values from 0 to 3
- dirichlet: int32 [64, 32, 1024], P('gx', 'gy', 'gz'), may hold values 0 or 1
- prony_moduli: float32 [4, 6], replicated, may hold values from 0.02 to 0.12
- prony_times: float32 [4, 6], replicated, may hold values from 0.05 to 50
- shear_modulus: float32 [4], replicated, may hold values from 0.5 to 2
- mullins_ratio: float32 [4], replicated, may hold values from 1.5 to 4
- mullins_scale: float32 [4], replicated, may hold values from 0.3 to 3
Outputs:
- stress: float32 [6, 64, 32, 1024], P(None, 'gx', 'gy', 'gz')
- visco_next: float32 [6, 6, 64, 32, 1024], P(None, None, 'gx', 'gy', 'gz')
- energy_next: float32 [64, 32, 1024], P('gx', 'gy', 'gz')
- damage_field: float32 [64, 32, 1024], P('gx', 'gy', 'gz')
- residual: float32 [64, 32, 1024], P('gx', 'gy', 'gz')
The draws below stay inside these ranges and needn't reach their ends.
All inputs are finite; a program needn't handle non-finite values. No bound on the sum of `dirichlet` on one device may be relied on, other than what follows from the above.
Results may differ from the reference program's by a relative error of at most 0.0003.
Values sent between devices are 32-bit elements; how exact they have to be, the bound alone decides.
A program may use at most 32 MiB of HBM per device.

```python
import math
import jax
import jax.numpy as jnp
from jax import lax

TERMS = 6
REGIONS = 4
ITERS = 4
NX = 64
NY = 32
NZ = 1024


def with_ends(entries, stream_key, least, top_value):
    extent = entries.shape
    spot = [jax.random.randint(jax.random.fold_in(stream_key, axis), (), 0, extent[axis]) for axis in range(len(extent))]
    entries = entries.at[tuple(spot)].set(least)
    longest = extent.index(max(extent))
    spot[longest] = (spot[longest] + 1) % extent[longest]
    return entries.at[tuple(spot)].set(top_value)


def levels(own_key, dims, shards, smallest, high):
    gain, own = 1.0, jax.random.fold_in(own_key, 6)
    for axis_at, shards_of in shards:
        heights = jnp.exp(jax.random.uniform(jax.random.fold_in(own, axis_at), (shards_of,), jnp.float32, smallest / len(shards), high / len(shards)))
        gain = gain * jnp.repeat(heights, dims[axis_at] // shards_of).reshape([-1 if axis == axis_at else 1 for axis in range(len(dims))])
    return gain


def normal_values(stream_key, extent, spread, most, split=(), held_as=jnp.bfloat16):
    result = spread * jax.random.normal(stream_key, extent, jnp.float32)
    if split:
        result = result * levels(stream_key, extent, split, -0.22, 0.18)
    return jnp.clip(result, -most, most).astype(held_as)


def setup_inputs(seed: int = 0) -> dict:
    seeds = jax.random.split(jax.random.key(seed), 12)
    return {
        "displacement": normal_values(seeds[0], (3, NX, NY, NZ), 1.0, 6.0, ((1, 32), (2, 4), (3, 8)), jnp.float32),
        "displacement_old": normal_values(seeds[1], (3, NX, NY, NZ), 1.0, 6.0, ((1, 32), (2, 4), (3, 8)), jnp.float32),
        "visco_state": normal_values(seeds[2], (TERMS, 6, NX, NY, NZ), 0.3, 3.0, ((2, 32), (3, 4), (4, 8)), jnp.float32),
        "energy_max": jnp.clip(jnp.exp(math.log(4.0) - 3.6888794 * jax.random.uniform(seeds[3], (NX, NY, NZ), jnp.float32) ** levels(seeds[3], (NX, NY, NZ), ((0, 32), (1, 4), (2, 8)), -0.2, 0.2)), 0.1, 4.0),
        "region": with_ends(jax.random.randint(seeds[4], (NX, NY, NZ), 0, REGIONS), jax.random.fold_in(seeds[4], 1), 0, REGIONS - 1).astype(jnp.int32),
        "dirichlet": with_ends((jax.random.randint(seeds[5], (NX, NY, NZ), 0, 8) < 1).astype(jnp.int32), jax.random.fold_in(seeds[5], 1), 0, 1),
        "prony_moduli": jnp.clip(jax.random.uniform(seeds[6], (REGIONS, TERMS), jnp.float32, 0.02, 0.12), 0.02, 0.12),
        "prony_times": jnp.clip(jnp.exp(jax.random.uniform(seeds[7], (REGIONS, TERMS), jnp.float32, math.log(0.05), math.log(50.0))), 0.05, 50.0),
        "shear_modulus": jnp.clip(jnp.exp(jax.random.uniform(seeds[8], (REGIONS,), jnp.float32, math.log(0.5), math.log(2.0))), 0.5, 2.0),
        "mullins_ratio": jnp.clip(jax.random.uniform(seeds[9], (REGIONS,), jnp.float32, 1.5, 4.0), 1.5, 4.0),
        "mullins_scale": jnp.clip(jnp.exp(jax.random.uniform(seeds[10], (REGIONS,), jnp.float32, math.log(0.3), math.log(3.0))), 0.3, 3.0),
    }


LENGTH_SQUARED = 4.0


def neighbours(field):
    next_x = jnp.roll(field, -1, axis=-3)
    prev_x = jnp.roll(field, 1, axis=-3)
    padding = [(0, 0)] * (field.ndim - 2) + [(1, 1), (1, 1)]
    padded = jnp.pad(field, padding)
    next_y = padded[..., 2:, 1:-1]
    prev_y = padded[..., :-2, 1:-1]
    next_z = padded[..., 1:-1, 2:]
    prev_z = padded[..., 1:-1, :-2]
    return next_x, prev_x, next_y, prev_y, next_z, prev_z


def deviator(held):
    next_x, prev_x, next_y, prev_y, next_z, prev_z = neighbours(held)
    grad_x = 0.5 * (next_x - prev_x)
    grad_y = 0.5 * (next_y - prev_y)
    grad_z = 0.5 * (next_z - prev_z)
    strain_xx = grad_x[0]
    strain_yy = grad_y[1]
    strain_zz = grad_z[2]
    strain_yz = 0.5 * (grad_z[1] + grad_y[2])
    strain_xz = 0.5 * (grad_z[0] + grad_x[2])
    strain_xy = 0.5 * (grad_y[0] + grad_x[1])
    trace_third = (strain_xx + strain_yy + strain_zz) / 3.0
    return jnp.stack([strain_xx - trace_third, strain_yy - trace_third, strain_zz - trace_third, strain_yz, strain_xz, strain_xy])


def contract(dev):
    return dev[0] * dev[0] + dev[1] * dev[1] + dev[2] * dev[2] + 2.0 * (dev[3] * dev[3] + dev[4] * dev[4] + dev[5] * dev[5])


def operate(field):
    next_x, prev_x, next_y, prev_y, next_z, prev_z = neighbours(field)
    beside_all = next_x + prev_x + next_y + prev_y + next_z + prev_z
    return (1.0 + 6.0 * LENGTH_SQUARED) * field - LENGTH_SQUARED * beside_all


def reference(displacement, displacement_old, visco_state, energy_max, region, dirichlet, prony_moduli, prony_times, shear_modulus, mullins_ratio, mullins_scale):
    free_share = (1 - dirichlet).astype(jnp.float32)
    dev_new = deviator(displacement * free_share[None])
    dev_old = deviator(displacement_old * free_share[None])
    shear_cells = shear_modulus[region]
    energy = shear_cells * contract(dev_new)
    energy_next = jnp.maximum(energy_max, energy)
    softening = 1.0 - jax.scipy.special.erf((energy_next - energy) / mullins_scale[region]) / mullins_ratio[region]
    stress_jump = 2.0 * shear_cells * (dev_new - dev_old)

    def prony_term(term_index):
        relax_time = prony_times[:, term_index][region]
        modulus = prony_moduli[:, term_index][region]
        decays = jnp.exp(-1.0 / relax_time)
        weight = modulus * (1.0 - decays) * relax_time
        return decays * visco_state[term_index] + weight * stress_jump

    visco_next = lax.map(prony_term, jnp.arange(TERMS))
    long_term = 1.0 - jnp.sum(prony_moduli, axis=1)[region]
    stress = softening * (long_term * 2.0 * shear_cells * dev_new + jnp.sum(visco_next, axis=0))
    local_drive = softening * energy

    damage_field = jnp.zeros_like(local_drive)
    residual = local_drive
    direction = local_drive
    norm_now = jnp.sum(residual * residual)
    for iteration in range(ITERS):
        image = operate(direction)
        alpha_now = norm_now / jnp.sum(direction * image)
        damage_field = damage_field + alpha_now * direction
        residual = residual - alpha_now * image
        norm_next = jnp.sum(residual * residual)
        direction = residual + (norm_next / norm_now) * direction
        norm_now = norm_next
    return stress, visco_next, energy_next, damage_field, residual
```

```python
import functools

import jax
import jax.numpy as jnp
from jax import lax
from jax.experimental import pallas as pl
from jax.experimental.pallas import tpu as pltpu
from jax.sharding import PartitionSpec as P

ITERS = 4
TERMS = 6
REGIONS = 4
SHIFTS = (1.0, 25.0, 25.0, 1.0)
PAIRS = tuple((i, j) for i in range(4) for j in range(i, 5))
F32 = jnp.float32


def deviator(grad):
    xx, yy, zz = grad[0][0], grad[1][1], grad[2][2]
    third = (xx + yy + zz) * (1.0 / 3.0)
    return (
        xx - third,
        yy - third,
        zz - third,
        0.5 * (grad[2][1] + grad[1][2]),
        0.5 * (grad[2][0] + grad[0][2]),
        0.5 * (grad[1][0] + grad[0][1]),
    )


def coefficients(gram):
    def form(left, right):
        total = None
        for i, a in enumerate(left):
            row = None
            for j, b in enumerate(right):
                term = b * gram[(min(i, j), max(i, j))]
                row = term if row is None else row + term
            row = a * row
            total = row if total is None else total + row
        return total

    one = jnp.ones_like(gram[(0, 0)])
    res, direction, field = [one], [one], []
    norm = gram[(0, 0)]
    for step in range(ITERS):
        image = []
        for k in range(step + 2):
            value = None
            if k <= step:
                value = SHIFTS[k] * direction[k]
            if k >= 1:
                value = 24.0 * direction[k - 1] if value is None else value + 24.0 * direction[k - 1]
            image.append(value)
        alpha = norm / form(direction, image)
        field = [field[k] + alpha * direction[k] if k < step else alpha * direction[k] for k in range(step + 1)]
        res = [res[k] - alpha * image[k] if k <= step else -alpha * image[k] for k in range(step + 2)]
        if step + 1 < ITERS:
            new = form(res, res)
            beta = new / norm
            direction = [res[k] + beta * direction[k] if k <= step else res[k] for k in range(step + 2)]
            norm = new
    return field, res


def kernel(sizes, *refs):
    nx, ny, nz, zhi = sizes
    low_n = nx // zhi
    line_n = zhi * nz
    plane_n = low_n * ny
    (disp_h, dold_h, visc_h, emax_h, reg_h, dir_h, moduli, times, shear, ratio, scale,
     stress_h, vnext_h, enext_h, field_h, resid_h,
     disp, dold, visc, emax, reg, dirm, stress, vnext, enext, field, resid,
     u, xr, ys, yr, zs, zr, e, eys, eyr, ezs, ezr, gs, gp, ts, tr,
     ld_sem, st_sem, ss, rs, ps_sem, pr_sem, ls_sem, lr_sem, dbl) = refs

    ix, iy, iz = lax.axis_index("gx"), lax.axis_index("gy"), lax.axis_index("gz")
    low, hi = ix % low_n, ix // low_n
    spot = hi * nz + iz
    place = low * ny + iy

    def on_x(d):
        return {"gx": (ix + d + nx) % nx, "gy": iy, "gz": iz}

    def on_y(d):
        return {"gx": ix, "gy": (iy + d + ny) % ny, "gz": iz}

    def on_line(d):
        q = (spot + d + line_n) % line_n
        return {"gx": (q // nz) * low_n + low, "gy": iy, "gz": q % nz}

    def on_plane(d):
        q = (place + d) % plane_n
        return {"gx": hi * low_n + q // ny, "gy": q % ny, "gz": iz}

    def signal(sem, dev):
        pl.semaphore_signal(sem, inc=1, device_id=dev, device_id_type=pl.DeviceIdType.MESH)

    def remote(src, dst, ssem, rsem, dev):
        return pltpu.make_async_remote_copy(
            src_ref=src, dst_ref=dst, send_sem=ssem, recv_sem=rsem,
            device_id=dev, device_id_type=pl.DeviceIdType.MESH)

    loads = [pltpu.make_async_copy(a, b, ld_sem.at[i]) for i, (a, b) in enumerate(
        ((dir_h, dirm), (disp_h, disp), (dold_h, dold), (reg_h, reg), (emax_h, emax), (visc_h, visc)))]
    for c in loads:
        c.start()

    barrier = pltpu.get_barrier_semaphore()
    greet = [on_x(2), on_x(-2), on_x(1), on_x(-1), on_line(1), on_line(-1)]
    greet += [on_plane(d) for d in range(1, plane_n)]
    for dev in greet:
        signal(barrier, dev)

    row = lax.broadcasted_iota(jnp.int32, (8, 128), 0)
    lane = lax.broadcasted_iota(jnp.int32, (8, 128), 1)
    ylo_on = jnp.where(iy > 0, 1.0, 0.0).astype(F32)
    yhi_on = jnp.where(iy < ny - 1, 1.0, 0.0).astype(F32)
    zlo_on = jnp.where(iz > 0, 1.0, 0.0).astype(F32)
    zhi_on = jnp.where(iz < nz - 1, 1.0, 0.0).astype(F32)

    loads[0].wait()
    loads[1].wait()
    loads[2].wait()
    zero = jnp.zeros((8, 128), F32)
    to_hi, to_lo = [zero, zero], [zero, zero]
    for half, src in enumerate((disp, dold)):
        for l in range(2):
            free = (1 - dirm[l]).astype(F32)
            for c in range(3):
                j = l * 3 + c
                val = src[c, l] * free
                u[half, l, c] = val
                ys[half, 0, j] = val[7:8]
                ys[half, 1, j] = val[0:1]
                to_hi[half] = jnp.where(lane == j, pltpu.roll(val, (j - 127) % 128, 1), to_hi[half])
                to_lo[half] = jnp.where(lane == j, pltpu.roll(val, j, 1) if j else val, to_lo[half])
        zs[half, 0] = to_hi[half]
        zs[half, 1] = to_lo[half]

    pl.semaphore_wait(barrier, len(greet))

    faces = []
    for half in range(2):
        faces.append([
            remote(u.at[half, 1], xr.at[half, 0], ss.at[half, 0], rs.at[half, 0], on_x(1)),
            remote(u.at[half, 0], xr.at[half, 1], ss.at[half, 1], rs.at[half, 1], on_x(-1)),
            remote(ys.at[half, 0], yr.at[half, 0], ss.at[half, 2], rs.at[half, 2], on_y(1)),
            remote(ys.at[half, 1], yr.at[half, 1], ss.at[half, 3], rs.at[half, 3], on_y(-1)),
            remote(zs.at[half, 0], zr.at[half, 0], ss.at[half, 4], rs.at[half, 4], on_line(1)),
            remote(zs.at[half, 1], zr.at[half, 1], ss.at[half, 5], rs.at[half, 5], on_line(-1)),
        ])
        for c in faces[half]:
            c.start()

    steps = []
    reach = 1
    while reach < line_n // 2:
        steps.append(reach)
        reach *= 2

    def dbl_signal(s):
        if s < len(steps):
            signal(dbl.at[s], on_line(steps[s]))
            signal(dbl.at[s], on_line(-steps[s]))

    def dbl_wait(s):
        if s < len(steps):
            pl.semaphore_wait(dbl.at[s], 2)

    dbl_signal(0)
    for s in range(len(steps) - 1):
        dbl_wait(s)
        dbl_signal(s + 1)

    loads[3].wait()
    loads[4].wait()

    def pick(table, where_is):
        out = table[REGIONS - 1]
        for k in range(REGIONS - 2, -1, -1):
            out = jnp.where(where_is[k], table[k], out)
        return out

    is_region = [[reg[l] == k for k in range(REGIONS)] for l in range(2)]
    shear_c = [pick([shear[k] for k in range(REGIONS)], is_region[l]) for l in range(2)]
    ratio_c = [pick([ratio[k] for k in range(REGIONS)], is_region[l]) for l in range(2)]
    scale_c = [pick([scale[k] for k in range(REGIONS)], is_region[l]) for l in range(2)]

    def strains(half):
        from_lo = zr[half, 0] * zlo_on
        from_hi = zr[half, 1] * zhi_on
        out = []
        for l in range(2):
            grad = [[None] * 3 for _ in range(3)]
            for c in range(3):
                j = l * 3 + c
                val = u[half, l, c]
                prev_x = xr[half, 0, c] if l == 0 else u[half, 0, c]
                next_x = xr[half, 1, c] if l == 1 else u[half, 1, c]
                below = jnp.broadcast_to(yr[half, 0, j] * ylo_on, (8, 128))
                above = jnp.broadcast_to(yr[half, 1, j] * yhi_on, (8, 128))
                prev_y = pltpu.roll(jnp.where(row == 7, below, val), 1, 0)
                next_y = pltpu.roll(jnp.where(row == 0, above, val), 7, 0)
                prev_z = jnp.where(lane == 0, pltpu.roll(from_lo, (128 - j) % 128, 1), pltpu.roll(val, 1, 1))
                next_z = jnp.where(lane == 127, pltpu.roll(from_hi, 127 - j, 1), pltpu.roll(val, 127, 1))
                grad[0][c] = 0.5 * (next_x - prev_x)
                grad[1][c] = 0.5 * (next_y - prev_y)
                grad[2][c] = 0.5 * (next_z - prev_z)
            out.append(deviator(grad))
        return out

    for c in faces[0]:
        c.wait_recv()
    dev_new = strains(0)
    softening = []
    for l in range(2):
        d = dev_new[l]
        energy = shear_c[l] * (
            d[0] * d[0] + d[1] * d[1] + d[2] * d[2] + 2.0 * (d[3] * d[3] + d[4] * d[4] + d[5] * d[5]))
        peak = jnp.maximum(emax[l], energy)
        soft = 1.0 - lax.erf((peak - energy) / scale_c[l]) / ratio_c[l]
        enext[l] = peak
        softening.append(soft)
        e[4 + l] = soft * energy

    own = e.at[pl.ds(4, 2)]
    wide = [
        remote(own, e.at[pl.ds(2, 2)], ss.at[2, 0], rs.at[2, 0], on_x(1)),
        remote(own, e.at[pl.ds(6, 2)], ss.at[2, 1], rs.at[2, 1], on_x(-1)),
        remote(own, e.at[pl.ds(0, 2)], ss.at[2, 2], rs.at[2, 2], on_x(2)),
        remote(own, e.at[pl.ds(8, 2)], ss.at[2, 3], rs.at[2, 3], on_x(-2)),
    ]
    for c in wide:
        c.start()

    for c in faces[1]:
        c.wait_recv()
    loads[5].wait()
    dev_old = strains(1)
    jump = [[2.0 * shear_c[l] * (dev_new[l][a] - dev_old[l][a]) for a in range(6)] for l in range(2)]
    total = [[None] * 6 for _ in range(2)]
    for k in range(TERMS):
        for l in range(2):
            tau = pick([times[r, k] for r in range(REGIONS)], is_region[l])
            mod = pick([moduli[r, k] for r in range(REGIONS)], is_region[l])
            decay = jnp.exp(-1.0 / tau)
            weight = mod * (1.0 - decay) * tau
            for a in range(6):
                val = decay * visc[k, a, l] + weight * jump[l][a]
                vnext[k, a, l] = val
                total[l][a] = val if k == 0 else total[l][a] + val
    for l in range(2):
        sums = []
        for r in range(REGIONS):
            s = moduli[r, 0]
            for k in range(1, TERMS):
                s = s + moduli[r, k]
            sums.append(1.0 - s)
        factor = pick(sums, is_region[l]) * 2.0 * shear_c[l]
        for a in range(6):
            stress[a, l] = softening[l] * (factor * dev_new[l][a] + total[l][a])
    stores = [pltpu.make_async_copy(a, b, st_sem.at[i]) for i, (a, b) in enumerate(
        ((vnext, vnext_h), (stress, stress_h), (enext, enext_h), (field, field_h), (resid, resid_h)))]
    for c in stores[:3]:
        c.start()

    for c in wide:
        c.wait_recv()
    for l in range(8):
        eys[0, l] = e[1 + l, 4:8]
        eys[1, l] = e[1 + l, 0:4]
    rows = [
        remote(eys.at[0], eyr.at[0], ss.at[3, 0], rs.at[3, 0], on_y(1)),
        remote(eys.at[1], eyr.at[1], ss.at[3, 1], rs.at[3, 1], on_y(-1)),
    ]
    for c in rows:
        c.start()
    row_mask = jnp.where(row < 4, yhi_on, ylo_on)
    lane_mask = jnp.where(lane < 4, zhi_on, jnp.where(lane >= 124, zlo_on, 0.0))
    masks = {(1, 0): row_mask, (0, 1): lane_mask, (1, 1): row_mask * lane_mask}
    to_hi, to_lo = zero, zero

    def pack(val, j, to_hi, to_lo):
        here = (lane >= 4 * j) & (lane < 4 * j + 4)
        to_hi = jnp.where(here, pltpu.roll(val, (4 * j - 124) % 128, 1), to_hi)
        to_lo = jnp.where(here, pltpu.roll(val, 4 * j, 1) if j else val, to_lo)
        return to_hi, to_lo

    basis = {}
    for l in range(10):
        basis[(l, 0, 0)] = e[l]
        if 1 <= l <= 8:
            to_hi, to_lo = pack(basis[(l, 0, 0)], (l - 1) * 2, to_hi, to_lo)
    for c in rows:
        c.wait_recv()
    for l in range(1, 9):
        val = jnp.concatenate([eyr[1, l - 1], eyr[0, l - 1]], axis=0) * row_mask
        basis[(l, 1, 0)] = val
        to_hi, to_lo = pack(val, (l - 1) * 2 + 1, to_hi, to_lo)
    ezs[0] = to_hi
    ezs[1] = to_lo
    cols = [
        remote(ezs.at[0], ezr.at[0], ss.at[3, 2], rs.at[3, 2], on_line(1)),
        remote(ezs.at[1], ezr.at[1], ss.at[3, 3], rs.at[3, 3], on_line(-1)),
    ]
    for c in cols:
        c.start()
    for c in cols:
        c.wait_recv()
    from_lo, from_hi = ezr[0], ezr[1]
    for l in range(1, 9):
        for t in range(2):
            j = (l - 1) * 2 + t
            val = jnp.where(lane < 4,
                            pltpu.roll(from_hi, (128 - 4 * j) % 128, 1),
                            pltpu.roll(from_lo, (124 - 4 * j) % 128, 1))
            basis[(l, t, 1)] = val * masks[(t, 1)]

    def grow(now, k):
        cache = {}

        def rolled(key, amount, axis):
            at = (key, amount, axis)
            if at not in cache:
                cache[at] = pltpu.roll(now[key], amount, axis)
            return cache[at]

        out = {}
        for l in range(k + 1, 9 - k):
            inner = k + 2 <= l <= 7 - k
            for ty, tz in ((0, 0), (1, 0), (0, 1), (1, 1)) if inner else ((0, 0),):
                me = (l, ty, tz)
                acc = now[(l - 1, ty, tz)] + now[(l + 1, ty, tz)]
                acc = acc + jnp.where(row == 7, rolled((l, 1 - ty, tz), 7, 0), rolled(me, 7, 0))
                acc = acc + jnp.where(row == 0, rolled((l, 1 - ty, tz), 1, 0), rolled(me, 1, 0))
                acc = acc + jnp.where(lane == 127, rolled((l, ty, 1 - tz), 127, 1), rolled(me, 127, 1))
                acc = acc + jnp.where(lane == 0, rolled((l, ty, 1 - tz), 1, 1), rolled(me, 1, 1))
                acc = acc * (1.0 / 6.0)
                acc = now[me] - acc if SHIFTS[k] == 1.0 else -acc
                if (ty, tz) != (0, 0):
                    acc = acc * masks[(ty, tz)]
                out[me] = acc
        return out

    powers = [basis]
    for k in range(ITERS):
        powers.append(grow(powers[-1], k))
    vecs = [[p[(4, 0, 0)], p[(5, 0, 0)]] for p in powers]

    sums = zero
    for n, (i, j) in enumerate(PAIRS):
        part = vecs[i][0] * vecs[j][0] + vecs[i][1] * vecs[j][1]
        sums = jnp.where(lane == n, jnp.sum(part, axis=1, keepdims=True), sums)
    mine = jnp.sum(sums, axis=0, keepdims=True)

    gs[0] = mine
    sends = []
    for d in range(1, plane_n):
        c = remote(gs.at[0], gp.at[d - 1], ps_sem, pr_sem, on_plane(d))
        c.start()
    every = remote(gp, gp, ps_sem, pr_sem, on_plane(1))
    every.wait_recv()
    acc = mine
    for d in range(plane_n - 1):
        acc = acc + gp[d]
    ts[0] = acc
    dbl_wait(len(steps) - 1)
    order = sorted(range(1, line_n), key=lambda d: -min(d, line_n - d))
    for d in order:
        c = remote(ts.at[0], tr.at[d - 1], ls_sem, lr_sem, on_line(d))
        c.start()
    along = remote(tr, tr, ls_sem, lr_sem, on_line(1))
    along.wait_recv()
    for d in range(line_n - 1):
        acc = acc + tr[d]

    full = jnp.broadcast_to(acc, (8, 128))
    gram = {pair: jnp.broadcast_to(full[:, n:n + 1], (8, 128)) for n, pair in enumerate(PAIRS)}
    on_field, on_resid = coefficients(gram)
    for l in range(2):
        val = on_field[0] * vecs[0][l]
        for k in range(1, ITERS):
            val = val + on_field[k] * vecs[k][l]
        field[l] = val
        val = on_resid[0] * vecs[0][l]
        for k in range(1, ITERS + 1):
            val = val + on_resid[k] * vecs[k][l]
        resid[l] = val
    for c in stores[3:]:
        c.start()
    for group in (faces[0], faces[1], wide, rows, cols):
        for c in group:
            c.wait_send()
    every.wait_send()
    along.wait_send()
    for c in stores:
        c.wait()


def solution(mesh):
    nx, ny, nz = mesh.shape["gx"], mesh.shape["gy"], mesh.shape["gz"]
    zhi = 4 if nx % 32 == 0 else 2
    low_n = nx // zhi
    line_n, plane_n = zhi * nz, low_n * ny

    def on_device(*args):
        hbm = pl.BlockSpec(memory_space=pl.ANY)
        smem = pl.BlockSpec(memory_space=pltpu.SMEM)
        outs = (
            jax.ShapeDtypeStruct((6, 2, 8, 128), F32),
            jax.ShapeDtypeStruct((6, 6, 2, 8, 128), F32),
            jax.ShapeDtypeStruct((2, 8, 128), F32),
            jax.ShapeDtypeStruct((2, 8, 128), F32),
            jax.ShapeDtypeStruct((2, 8, 128), F32),
        )
        vm = pltpu.VMEM
        dma = pltpu.SemaphoreType.DMA
        return pl.pallas_call(
            functools.partial(kernel, (nx, ny, nz, zhi)),
            out_shape=outs,
            in_specs=[hbm] * 6 + [smem] * 5,
            out_specs=[hbm] * 5,
            scratch_shapes=[
                vm((3, 2, 8, 128), F32), vm((3, 2, 8, 128), F32), vm((6, 6, 2, 8, 128), F32),
                vm((2, 8, 128), F32), vm((2, 8, 128), jnp.int32), vm((2, 8, 128), jnp.int32),
                vm((6, 2, 8, 128), F32), vm((6, 6, 2, 8, 128), F32),
                vm((2, 8, 128), F32), vm((2, 8, 128), F32), vm((2, 8, 128), F32),
                vm((2, 2, 3, 8, 128), F32), vm((2, 2, 3, 8, 128), F32),
                vm((2, 2, 6, 1, 128), F32), vm((2, 2, 6, 1, 128), F32),
                vm((2, 2, 8, 128), F32), vm((2, 2, 8, 128), F32),
                vm((10, 8, 128), F32),
                vm((2, 8, 4, 128), F32), vm((2, 8, 4, 128), F32),
                vm((2, 8, 128), F32), vm((2, 8, 128), F32),
                vm((1, 1, 128), F32), vm((plane_n - 1, 1, 128), F32),
                vm((1, 1, 128), F32), vm((line_n - 1, 1, 128), F32),
                dma((6,)), dma((5,)), dma((4, 6)), dma((4, 6)), dma, dma, dma, dma,
                pltpu.SemaphoreType.REGULAR((4,)),
            ],
            compiler_params=pltpu.CompilerParams(collective_id=0, has_side_effects=True),
        )(*args)

    cell = P("gx", "gy", "gz")
    vec = P(None, "gx", "gy", "gz")
    ten = P(None, None, "gx", "gy", "gz")
    return jax.shard_map(
        on_device,
        mesh=mesh,
        in_specs=(vec, vec, ten, cell, cell, cell, P(), P(), P(), P(), P()),
        out_specs=(vec, ten, cell, cell, cell),
        check_vma=False,
    )
```

```python
import functools

import jax
import jax.numpy as jnp
from jax import lax
from jax.experimental import pallas as pl
from jax.experimental.pallas import tpu as pltpu
from jax.sharding import PartitionSpec as P

ITERS = 4
TERMS = 6
REGIONS = 4
SHIFTS = (1.0, 25.0, 25.0, 1.0)
PAIRS = tuple((i, j) for i in range(4) for j in range(i, 5))
F32 = jnp.float32


def deviator(grad):
    xx, yy, zz = grad[0][0], grad[1][1], grad[2][2]
    third = (xx + yy + zz) * (1.0 / 3.0)
    return (
        xx - third,
        yy - third,
        zz - third,
        0.5 * (grad[2][1] + grad[1][2]),
        0.5 * (grad[2][0] + grad[0][2]),
        0.5 * (grad[1][0] + grad[0][1]),
    )


def coefficients(gram):
    def form(left, right):
        total = None
        for i, a in enumerate(left):
            row = None
            for j, b in enumerate(right):
                term = b * gram[(min(i, j), max(i, j))]
                row = term if row is None else row + term
            row = a * row
            total = row if total is None else total + row
        return total

    one = jnp.ones_like(gram[(0, 0)])
    res, direction, field = [one], [one], []
    norm = gram[(0, 0)]
    for step in range(ITERS):
        image = []
        for k in range(step + 2):
            value = None
            if k <= step:
                value = SHIFTS[k] * direction[k]
            if k >= 1:
                value = 24.0 * direction[k - 1] if value is None else value + 24.0 * direction[k - 1]
            image.append(value)
        alpha = norm / form(direction, image)
        field = [field[k] + alpha * direction[k] if k < step else alpha * direction[k] for k in range(step + 1)]
        res = [res[k] - alpha * image[k] if k <= step else -alpha * image[k] for k in range(step + 2)]
        if step + 1 < ITERS:
            new = form(res, res)
            beta = new / norm
            direction = [res[k] + beta * direction[k] if k <= step else res[k] for k in range(step + 2)]
            norm = new
    return field, res


def kernel(sizes, *refs):
    nx, ny, nz, zhi = sizes
    low_n = nx // zhi
    line_n = zhi * nz
    plane_n = low_n * ny
    half_way = nz // 2
    (disp_h, dold_h, visc_h, emax_h, reg_h, dir_h, moduli_h, times_h, shear_h, ratio_h, scale_h,
     stress, vnext, enext, vout, sums_out,
     disp, dold, visc, emax, reg, dirm, moduli, times, shear, ratio, scale,
     u, xr, ys, yr, zs, zr, e, eys, eyr, ezs, ezr, gs, gp, ts, tr,
     ld_sem, ss, rs, ps_sem, pr_sem, ls_sem, lr_sem, dbl, xok) = refs

    ix, iy, iz = lax.axis_index("gx"), lax.axis_index("gy"), lax.axis_index("gz")
    low, hi = ix % low_n, ix // low_n
    spot = hi * nz + iz
    place = low * ny + iy
    top = low == low_n - 1
    bottom = low == 0

    def on_x(d):
        return {"gx": (ix + d + nx) % nx, "gy": iy, "gz": iz}

    def at(d, low_to, dy=0):
        q = (spot + d + line_n) % line_n
        return {"gx": (q // nz) * low_n + low_to, "gy": (iy + dy + ny) % ny, "gz": q % nz}

    def on_line(d, dy=0):
        return at(d, low, dy)

    def on_plane(d):
        q = (place + d) % plane_n
        return {"gx": hi * low_n + q // ny, "gy": q % ny, "gz": iz}

    def either(cond, one, other):
        return {k: jnp.where(cond, one[k], other[k]) for k in one}

    def signal(sem, dev):
        pl.semaphore_signal(sem, inc=1, device_id=dev, device_id_type=pl.DeviceIdType.MESH)

    def remote(src, dst, ssem, rsem, dev):
        return pltpu.make_async_remote_copy(
            src_ref=src, dst_ref=dst, send_sem=ssem, recv_sem=rsem,
            device_id=dev, device_id_type=pl.DeviceIdType.MESH)

    loads = [pltpu.make_async_copy(a, b, ld_sem.at[i]) for i, (a, b) in enumerate(
        ((dir_h, dirm), (disp_h, disp), (dold_h, dold), (reg_h, reg), (emax_h, emax),
         (shear_h, shear), (ratio_h, ratio), (scale_h, scale), (moduli_h, moduli), (times_h, times),
         (visc_h, visc)))]
    for c in loads[:2]:
        c.start()

    barrier = pltpu.get_barrier_semaphore()
    mirror = low_n - 1 - low
    greet = [at(half_way, mirror), at(-half_way, mirror), on_line(half_way), on_line(-half_way)]
    greet += [on_plane(d) for d in range(1, plane_n)]
    greet += [on_line(1), on_line(-1)]
    for dev in greet:
        signal(barrier, dev)
    for c in loads[2:]:
        c.start()

    row = lax.broadcasted_iota(jnp.int32, (8, 128), 0)
    lane = lax.broadcasted_iota(jnp.int32, (8, 128), 1)
    ylo_on = jnp.where(iy > 0, 1.0, 0.0).astype(F32)
    yhi_on = jnp.where(iy < ny - 1, 1.0, 0.0).astype(F32)
    zlo_on = jnp.where(iz > 0, 1.0, 0.0).astype(F32)
    zhi_on = jnp.where(iz < nz - 1, 1.0, 0.0).astype(F32)

    def hold(half, src):
        to_hi, to_lo = zero, zero
        for l in range(2):
            free = (1 - dirm[l]).astype(F32)
            for c in range(3):
                j = l * 3 + c
                val = src[c, l] * free
                u[half, l, c] = val
                ys[half, 0, j] = val[7:8]
                ys[half, 1, j] = val[0:1]
                to_hi = jnp.where(lane == j, pltpu.roll(val, (j - 127) % 128, 1), to_hi)
                to_lo = jnp.where(lane == j, pltpu.roll(val, j, 1) if j else val, to_lo)
        zs[half, 0] = to_hi
        zs[half, 1] = to_lo

    def send_faces(half):
        out = [
            remote(u.at[half, 1], xr.at[half, jnp.where(top, 2, 0)], ss.at[half, 0],
                   rs.at[half, jnp.where(top, 6, 0)], either(top, on_line(half_way), on_x(1))),
            remote(u.at[half, 0], xr.at[half, jnp.where(bottom, 2, 1)], ss.at[half, 1],
                   rs.at[half, jnp.where(bottom, 6, 1)], either(bottom, on_line(-half_way), on_x(-1))),
            remote(ys.at[half, 0], yr.at[half, 0], ss.at[half, 2], rs.at[half, 2], on_line(0, 1)),
            remote(ys.at[half, 1], yr.at[half, 1], ss.at[half, 3], rs.at[half, 3], on_line(0, -1)),
            remote(zs.at[half, 0], zr.at[half, 0], ss.at[half, 4], rs.at[half, 4], on_line(1)),
            remote(zs.at[half, 1], zr.at[half, 1], ss.at[half, 5], rs.at[half, 5], on_line(-1)),
        ]
        for c in out:
            c.start()
        return out

    def relay(half):
        side = jnp.where(top, 0, 1)
        return remote(xr.at[half, 2], xr.at[half, side], ss.at[half, 6], rs.at[half, side],
                      either(top, at(half_way, 0), at(-half_way, low_n - 1)))

    def pass_on(half):
        @pl.when(top | bottom)
        def _():
            remote(xr.at[half, 2], xr.at[half, 2], ss.at[half, 6], rs.at[half, 6], on_line(1)).wait_recv()
            relay(half).start()

    def wait_faces(half):
        for i, dst in enumerate((xr.at[half, 0], xr.at[half, 1], yr.at[half, 0], yr.at[half, 1],
                                 zr.at[half, 0], zr.at[half, 1])):
            remote(dst, dst, ss.at[half, i], rs.at[half, i], on_line(1)).wait_recv()

    zero = jnp.zeros((8, 128), F32)
    loads[0].wait()
    loads[1].wait()
    hold(0, disp)
    pl.semaphore_wait(barrier, len(greet))
    faces = [send_faces(0)]

    steps = []
    reach = 1
    while reach < line_n // 2:
        steps.append(reach)
        reach *= 2

    def dbl_signal(s):
        if s < len(steps):
            signal(dbl.at[s], on_line(steps[s]))
            signal(dbl.at[s], on_line(-steps[s]))

    known = set()

    def dbl_wait(s):
        if s < len(steps) and s not in known:
            known.add(s)
            pl.semaphore_wait(dbl.at[s], 2)

    dbl_signal(0)
    for c in loads[2:10]:
        c.wait()
    hold(1, dold)
    dbl_wait(0)
    dbl_signal(1)
    pass_on(0)

    def pick(table, where_is):
        out = table[REGIONS - 1]
        for k in range(REGIONS - 2, -1, -1):
            out = jnp.where(where_is[k], table[k], out)
        return out

    is_region = [[reg[l] == k for k in range(REGIONS)] for l in range(2)]
    shear_c = [pick([shear[k] for k in range(REGIONS)], is_region[l]) for l in range(2)]
    ratio_c = [pick([ratio[k] for k in range(REGIONS)], is_region[l]) for l in range(2)]
    scale_c = [pick([scale[k] for k in range(REGIONS)], is_region[l]) for l in range(2)]

    def strains(half):
        from_lo = zr[half, 0] * zlo_on
        from_hi = zr[half, 1] * zhi_on
        out = []
        for l in range(2):
            grad = [[None] * 3 for _ in range(3)]
            for c in range(3):
                j = l * 3 + c
                val = u[half, l, c]
                prev_x = xr[half, 0, c] if l == 0 else u[half, 0, c]
                next_x = xr[half, 1, c] if l == 1 else u[half, 1, c]
                below = jnp.broadcast_to(yr[half, 0, j] * ylo_on, (8, 128))
                above = jnp.broadcast_to(yr[half, 1, j] * yhi_on, (8, 128))
                prev_y = pltpu.roll(jnp.where(row == 7, below, val), 1, 0)
                next_y = pltpu.roll(jnp.where(row == 0, above, val), 7, 0)
                prev_z = jnp.where(lane == 0, pltpu.roll(from_lo, (128 - j) % 128, 1), pltpu.roll(val, 1, 1))
                next_z = jnp.where(lane == 127, pltpu.roll(from_hi, 127 - j, 1), pltpu.roll(val, 127, 1))
                grad[0][c] = 0.5 * (next_x - prev_x)
                grad[1][c] = 0.5 * (next_y - prev_y)
                grad[2][c] = 0.5 * (next_z - prev_z)
            out.append(deviator(grad))
        return out

    wait_faces(0)

    @pl.when(top)
    def _():
        signal(xok, on_x(-1))

    @pl.when(bottom)
    def _():
        signal(xok, on_x(1))

    dev_new = strains(0)
    softening = []
    for l in range(2):
        d = dev_new[l]
        energy = shear_c[l] * (
            d[0] * d[0] + d[1] * d[1] + d[2] * d[2] + 2.0 * (d[3] * d[3] + d[4] * d[4] + d[5] * d[5]))
        peak = jnp.maximum(emax[l], energy)
        soft = 1.0 - lax.erf((peak - energy) / scale_c[l]) / ratio_c[l]
        enext[l] = peak
        softening.append(soft)
        e[4 + l] = soft * energy

    own = e.at[pl.ds(4, 2)]
    wide = [
        remote(own, e.at[pl.ds(2, 2)], ss.at[2, 0], rs.at[2, 0], on_x(1)),
        remote(own, e.at[pl.ds(6, 2)], ss.at[2, 1], rs.at[2, 1], on_x(-1)),
        remote(own, e.at[pl.ds(0, 2)], ss.at[2, 2], rs.at[2, 2], on_x(2)),
        remote(own, e.at[pl.ds(8, 2)], ss.at[2, 3], rs.at[2, 3], on_x(-2)),
    ]
    for c in wide[:2]:
        c.start()

    @pl.when((low == low_n - 2) | (low == 1))
    def _():
        pl.semaphore_wait(xok, 1)

    for c in wide[2:]:
        c.start()
    faces.append(send_faces(1))
    dbl_wait(1)
    dbl_signal(2)
    pass_on(1)
    dbl_wait(2)
    dbl_signal(3)


    row_mask = jnp.where(row < 4, yhi_on, ylo_on)
    lane_mask = jnp.where(lane < 4, zhi_on, jnp.where(lane >= 124, zlo_on, 0.0))
    masks = {(1, 0): row_mask, (0, 1): lane_mask, (1, 1): row_mask * lane_mask}
    to_hi, to_lo = zero, zero
    basis = {}
    for l in (4, 5, 2, 3, 6, 7, 0, 1, 8, 9):
        if l in (2, 6, 0, 8):
            wide[(2, 6, 0, 8).index(l)].wait_recv()
        val = e[l]
        basis[(l, 0, 0)] = val
        if 1 <= l <= 8:
            j = l - 1
            eys[0, j] = val[4:8]
            eys[1, j] = val[0:4]
            here = (lane >= 4 * j) & (lane < 4 * j + 4)
            to_hi = jnp.where(here, pltpu.roll(val, (4 * j - 124) % 128, 1), to_hi)
            to_lo = jnp.where(here, pltpu.roll(val, 4 * j, 1) if j else val, to_lo)
    ezs[0] = to_hi
    ezs[1] = to_lo
    edges = [
        remote(ezs.at[0], ezr.at[2], ss.at[3, 0], rs.at[3, 0], on_line(1, 1)),
        remote(ezs.at[0], ezr.at[3], ss.at[3, 1], rs.at[3, 1], on_line(1, -1)),
        remote(ezs.at[1], ezr.at[4], ss.at[3, 2], rs.at[3, 2], on_line(-1, 1)),
        remote(ezs.at[1], ezr.at[5], ss.at[3, 3], rs.at[3, 3], on_line(-1, -1)),
        remote(ezs.at[0], ezr.at[0], ss.at[3, 4], rs.at[3, 4], on_line(1)),
        remote(ezs.at[1], ezr.at[1], ss.at[3, 5], rs.at[3, 5], on_line(-1)),
        remote(eys.at[0], eyr.at[0], ss.at[3, 6], rs.at[3, 6], on_line(0, 1)),
        remote(eys.at[1], eyr.at[1], ss.at[3, 7], rs.at[3, 7], on_line(0, -1)),
    ]
    for c in edges:
        c.start()
    for c in edges[6:]:
        c.wait_recv()
    for l in range(1, 9):
        basis[(l, 1, 0)] = jnp.concatenate([eyr[1, l - 1], eyr[0, l - 1]], axis=0) * row_mask
    for c in edges[:6]:
        c.wait_recv()
    sides = ((ezr[0], ezr[1]),
             (jnp.where(row < 4, ezr[3], ezr[2]), jnp.where(row < 4, ezr[5], ezr[4])))
    for l in range(1, 9):
        for t in range(2):
            j = l - 1
            from_lo, from_hi = sides[t]
            val = jnp.where(lane < 4,
                            pltpu.roll(from_hi, 128 - 4 * j, 1) if j else from_hi,
                            pltpu.roll(from_lo, 124 - 4 * j, 1))
            basis[(l, t, 1)] = val * masks[(t, 1)]

    def grow(now, k):
        cache = {}

        def rolled(key, amount, axis):
            at = (key, amount, axis)
            if at not in cache:
                cache[at] = pltpu.roll(now[key], amount, axis)
            return cache[at]

        out = {}
        for l in range(k + 1, 9 - k):
            inner = k + 2 <= l <= 7 - k
            for ty, tz in ((0, 0), (1, 0), (0, 1), (1, 1)) if inner else ((0, 0),):
                me = (l, ty, tz)
                acc = now[(l - 1, ty, tz)] + now[(l + 1, ty, tz)]
                acc = acc + jnp.where(row == 7, rolled((l, 1 - ty, tz), 7, 0), rolled(me, 7, 0))
                acc = acc + jnp.where(row == 0, rolled((l, 1 - ty, tz), 1, 0), rolled(me, 1, 0))
                acc = acc + jnp.where(lane == 127, rolled((l, ty, 1 - tz), 127, 1), rolled(me, 127, 1))
                acc = acc + jnp.where(lane == 0, rolled((l, ty, 1 - tz), 1, 1), rolled(me, 1, 1))
                acc = acc * (1.0 / 6.0)
                acc = now[me] - acc if SHIFTS[k] == 1.0 else -acc
                if (ty, tz) != (0, 0):
                    acc = acc * masks[(ty, tz)]
                out[me] = acc
        return out

    powers = [basis]
    for k in range(ITERS):
        powers.append(grow(powers[-1], k))
    vecs = [[p[(4, 0, 0)], p[(5, 0, 0)]] for p in powers]

    for k in range(ITERS + 1):
        for l in range(2):
            vout[2 * k + l] = vecs[k][l]
    sums = zero
    for n, (i, j) in enumerate(PAIRS):
        part = vecs[i][0] * vecs[j][0] + vecs[i][1] * vecs[j][1]
        sums = jnp.where(lane == n, jnp.sum(part, axis=1, keepdims=True), sums)
    mine = jnp.sum(sums, axis=0, keepdims=True)

    gs[0] = mine
    sends = []
    for d in range(1, plane_n):
        c = remote(gs.at[0], gp.at[d - 1], ps_sem, pr_sem, on_plane(d))
        c.start()
    every = remote(gp, gp, ps_sem, pr_sem, on_plane(1))
    every.wait_recv()
    acc = mine
    for d in range(plane_n - 1):
        acc = acc + gp[d]
    ts[0] = acc
    dbl_wait(len(steps) - 1)
    order = sorted(range(1, line_n), key=lambda d: -min(d, line_n - d))
    for d in order:
        c = remote(ts.at[0], tr.at[d - 1], ls_sem, lr_sem, on_line(d))
        c.start()
    wait_faces(1)
    loads[10].wait()
    dev_old = strains(1)
    jump = [[2.0 * shear_c[l] * (dev_new[l][a] - dev_old[l][a]) for a in range(6)] for l in range(2)]
    total = [[None] * 6 for _ in range(2)]
    for k in range(TERMS):
        for l in range(2):
            tau = pick([times[r, k] for r in range(REGIONS)], is_region[l])
            mod = pick([moduli[r, k] for r in range(REGIONS)], is_region[l])
            decay = jnp.exp(-1.0 / tau)
            weight = mod * (1.0 - decay) * tau
            for a in range(6):
                val = decay * visc[k, a, l] + weight * jump[l][a]
                vnext[k, a, l] = val
                total[l][a] = val if k == 0 else total[l][a] + val
    for l in range(2):
        sums = []
        for r in range(REGIONS):
            s = moduli[r, 0]
            for k in range(1, TERMS):
                s = s + moduli[r, k]
            sums.append(1.0 - s)
        factor = pick(sums, is_region[l]) * 2.0 * shear_c[l]
        for a in range(6):
            stress[a, l] = softening[l] * (factor * dev_new[l][a] + total[l][a])

    along = remote(tr, tr, ls_sem, lr_sem, on_line(1))
    along.wait_recv()
    for d in range(line_n - 1):
        acc = acc + tr[d]
    sums_out[...] = acc

    for group in (faces[0], faces[1], wide, edges):
        for c in group:
            c.wait_send()

    @pl.when(top | bottom)
    def _():
        relay(0).wait_send()
        relay(1).wait_send()

    every.wait_send()
    along.wait_send()


def finish(stress, vnext, enext, vecs, sums, stress_h, vnext_h, enext_h, field_h, resid_h, field, resid, sem):
    stores = [pltpu.make_async_copy(a, b, sem.at[i]) for i, (a, b) in enumerate(
        ((vnext, vnext_h), (stress, stress_h), (enext, enext_h), (field, field_h), (resid, resid_h)))]
    for c in stores[:3]:
        c.start()
    full = jnp.broadcast_to(sums[...], (8, 128))
    gram = {pair: jnp.broadcast_to(full[:, n:n + 1], (8, 128)) for n, pair in enumerate(PAIRS)}
    on_field, on_resid = coefficients(gram)
    for l in range(2):
        val = on_field[0] * vecs[l]
        for k in range(1, ITERS):
            val = val + on_field[k] * vecs[2 * k + l]
        field[l] = val
        val = on_resid[0] * vecs[l]
        for k in range(1, ITERS + 1):
            val = val + on_resid[k] * vecs[2 * k + l]
        resid[l] = val
    for c in stores[3:]:
        c.start()
    for c in stores:
        c.wait()


def solution(mesh):
    nx, ny, nz = mesh.shape["gx"], mesh.shape["gy"], mesh.shape["gz"]
    zhi = 4 if nx % 32 == 0 else 2
    low_n = nx // zhi
    line_n, plane_n = zhi * nz, low_n * ny

    def on_device(*args):
        hbm = pl.BlockSpec(memory_space=pltpu.HBM)
        local = pl.BlockSpec(memory_space=pltpu.VMEM)
        vm = pltpu.VMEM
        sm = pltpu.SMEM
        dma = pltpu.SemaphoreType.DMA
        cells = jax.ShapeDtypeStruct((2, 8, 128), F32)
        stress = jax.ShapeDtypeStruct((6, 2, 8, 128), F32)
        visco = jax.ShapeDtypeStruct((6, 6, 2, 8, 128), F32)
        parts = pl.pallas_call(
            functools.partial(kernel, (nx, ny, nz, zhi)),
            out_shape=(stress, visco, cells,
                       jax.ShapeDtypeStruct((10, 8, 128), F32), jax.ShapeDtypeStruct((1, 128), F32)),
            in_specs=[hbm] * 11,
            out_specs=[local] * 5,
            scratch_shapes=[
                vm((3, 2, 8, 128), F32), vm((3, 2, 8, 128), F32), vm((6, 6, 2, 8, 128), F32),
                vm((2, 8, 128), F32), vm((2, 8, 128), jnp.int32), vm((2, 8, 128), jnp.int32),
                sm((4, 6), F32), sm((4, 6), F32), sm((4,), F32), sm((4,), F32), sm((4,), F32),
                vm((2, 2, 3, 8, 128), F32), vm((2, 3, 3, 8, 128), F32),
                vm((2, 2, 6, 1, 128), F32), vm((2, 2, 6, 1, 128), F32),
                vm((2, 2, 8, 128), F32), vm((2, 2, 8, 128), F32),
                vm((10, 8, 128), F32),
                vm((2, 8, 4, 128), F32), vm((2, 8, 4, 128), F32),
                vm((2, 8, 128), F32), vm((6, 8, 128), F32),
                vm((1, 1, 128), F32), vm((plane_n - 1, 1, 128), F32),
                vm((1, 1, 128), F32), vm((line_n - 1, 1, 128), F32),
                dma((11,)), dma((4, 8)), dma((4, 8)), dma, dma, dma, dma,
                pltpu.SemaphoreType.REGULAR((4,)), pltpu.SemaphoreType.REGULAR,
            ],
            compiler_params=pltpu.CompilerParams(
                collective_id=0, has_side_effects=True, vmem_limit_bytes=16 << 20),
        )(*[pltpu.with_memory_space_constraint(a, pltpu.HBM) for a in args])
        return pl.pallas_call(
            finish,
            out_shape=(stress, visco, cells, cells, cells),
            in_specs=[local] * 5,
            out_specs=[hbm] * 5,
            scratch_shapes=[vm((2, 8, 128), F32), vm((2, 8, 128), F32), dma((5,))],
            compiler_params=pltpu.CompilerParams(vmem_limit_bytes=16 << 20),
        )(*parts)

    cell = P("gx", "gy", "gz")
    vec = P(None, "gx", "gy", "gz")
    ten = P(None, None, "gx", "gy", "gz")
    return jax.shard_map(
        on_device,
        mesh=mesh,
        in_specs=(vec, vec, ten, cell, cell, cell, P(), P(), P(), P(), P()),
        out_specs=(vec, ten, cell, cell, cell),
        check_vma=False,
    )
```

```python
import functools

import jax
import jax.numpy as jnp
from jax import lax
from jax.experimental import pallas as pl
from jax.experimental.pallas import tpu as pltpu
from jax.sharding import PartitionSpec as P

ITERS = 4
TERMS = 6
REGIONS = 4
SHIFTS = (1.0, 25.0, 25.0, 1.0)
PAIRS = tuple((i, j) for i in range(4) for j in range(i, 5))
F32 = jnp.float32


def flat_parts(grad_y, grad_z):
    return (grad_y[1], grad_z[2], 0.5 * (grad_z[1] + grad_y[2]), grad_z[0], grad_y[0])


def deviator(grad_x, flat):
    xx, yy, zz = grad_x[0], flat[0], flat[1]
    third = (xx + yy + zz) * (1.0 / 3.0)
    return (
        xx - third,
        yy - third,
        zz - third,
        flat[2],
        0.5 * (flat[3] + grad_x[2]),
        0.5 * (flat[4] + grad_x[1]),
    )


def coefficients(gram):
    def form(left, right):
        total = None
        for i, a in enumerate(left):
            row = None
            for j, b in enumerate(right):
                term = b * gram[(min(i, j), max(i, j))]
                row = term if row is None else row + term
            row = a * row
            total = row if total is None else total + row
        return total

    one = jnp.ones_like(gram[(0, 0)])
    res, direction, field = [one], [one], []
    norm = gram[(0, 0)]
    for step in range(ITERS):
        image = []
        for k in range(step + 2):
            value = None
            if k <= step:
                value = SHIFTS[k] * direction[k]
            if k >= 1:
                value = 24.0 * direction[k - 1] if value is None else value + 24.0 * direction[k - 1]
            image.append(value)
        alpha = norm / form(direction, image)
        field = [field[k] + alpha * direction[k] if k < step else alpha * direction[k] for k in range(step + 1)]
        res = [res[k] - alpha * image[k] if k <= step else -alpha * image[k] for k in range(step + 2)]
        if step + 1 < ITERS:
            new = form(res, res)
            beta = new / norm
            direction = [res[k] + beta * direction[k] if k <= step else res[k] for k in range(step + 2)]
            norm = new
    return field, res


def kernel(sizes, *refs):
    nx, ny, nz, zhi = sizes
    low_n = nx // zhi
    line_n = zhi * nz
    plane_n = low_n * ny
    half_way = nz // 2
    (disp_h, dold_h, visc_h, emax_h, reg_h, dir_h, moduli_h, times_h, shear_h, ratio_h, scale_h,
     stress, vnext, enext, vout, sums_out,
     disp, dold, visc, emax, reg, dirm, moduli, times, shear, ratio, scale,
     u, xr, ys, yr, zs, zr, e, eys, eyr, ezs, ezr, gs, gp, ts, tr,
     pk, mk, mu, ld_sem, ss, rs, ps_sem, pr_sem, ls_sem, lr_sem, dbl) = refs

    ix, iy, iz = lax.axis_index("gx"), lax.axis_index("gy"), lax.axis_index("gz")
    low, hi = ix % low_n, ix // low_n
    spot = hi * nz + iz
    place = low * ny + iy
    top = low == low_n - 1
    bottom = low == 0

    def on_x(d):
        return {"gx": (ix + d + nx) % nx, "gy": iy, "gz": iz}

    def at(d, low_to, dy=0):
        q = (spot + d + line_n) % line_n
        return {"gx": (q // nz) * low_n + low_to, "gy": (iy + dy + ny) % ny, "gz": q % nz}

    def on_line(d, dy=0):
        return at(d, low, dy)

    def on_plane(d):
        q = (place + d) % plane_n
        return {"gx": hi * low_n + q // ny, "gy": q % ny, "gz": iz}

    def either(cond, one, other):
        return {k: jnp.where(cond, one[k], other[k]) for k in one}

    def signal(sem, dev):
        pl.semaphore_signal(sem, inc=1, device_id=dev, device_id_type=pl.DeviceIdType.MESH)

    def remote(src, dst, ssem, rsem, dev):
        return pltpu.make_async_remote_copy(
            src_ref=src, dst_ref=dst, send_sem=ssem, recv_sem=rsem,
            device_id=dev, device_id_type=pl.DeviceIdType.MESH)

    loads = [pltpu.make_async_copy(a, b, ld_sem.at[i]) for i, (a, b) in enumerate(
        ((dir_h, dirm), (disp_h, disp), (dold_h, dold), (reg_h, reg), (emax_h, emax),
         (shear_h, shear), (ratio_h, ratio), (scale_h, scale), (moduli_h, moduli), (times_h, times),
         (visc_h, visc)))]
    for c in loads[:2]:
        c.start()

    barrier = pltpu.get_barrier_semaphore()
    greet = [at(s, (low + r + low_n) % low_n) for r in (0, 1, -1, 2, -2) for s in (half_way, -half_way)]
    greet += [on_plane(d) for d in range(1, plane_n)]
    greet += [on_line(1), on_line(-1)]
    for dev in greet:
        signal(barrier, dev)
    for c in loads[2:]:
        c.start()

    row = lax.broadcasted_iota(jnp.int32, (8, 128), 0)
    lane = lax.broadcasted_iota(jnp.int32, (8, 128), 1)
    ylo_on = jnp.where(iy > 0, 1.0, 0.0).astype(F32)
    yhi_on = jnp.where(iy < ny - 1, 1.0, 0.0).astype(F32)
    zlo_on = jnp.where(iz > 0, 1.0, 0.0).astype(F32)
    zhi_on = jnp.where(iz < nz - 1, 1.0, 0.0).astype(F32)

    def hold(half, src):
        to_hi, to_lo = zero, zero
        for l in range(2):
            free = (1 - dirm[l]).astype(F32)
            for c in range(3):
                j = l * 3 + c
                val = src[c, l] * free
                u[half, l, c] = val
                ys[half, 0, j] = val[7:8]
                ys[half, 1, j] = val[0:1]
                to_hi = jnp.where(lane == j, pltpu.roll(val, (j - 127) % 128, 1), to_hi)
                to_lo = jnp.where(lane == j, pltpu.roll(val, j, 1) if j else val, to_lo)
        zs[half, 0] = to_hi
        zs[half, 1] = to_lo

    def send_faces(half):
        out = [
            remote(u.at[half, 1], xr.at[half, jnp.where(top, 2, 0)], ss.at[half, 0],
                   rs.at[half, jnp.where(top, 6, 0)], either(top, on_line(half_way), on_x(1))),
            remote(u.at[half, 0], xr.at[half, jnp.where(bottom, 2, 1)], ss.at[half, 1],
                   rs.at[half, jnp.where(bottom, 6, 1)], either(bottom, on_line(-half_way), on_x(-1))),
            remote(ys.at[half, 0], yr.at[half, 0], ss.at[half, 2], rs.at[half, 2], on_line(0, 1)),
            remote(ys.at[half, 1], yr.at[half, 1], ss.at[half, 3], rs.at[half, 3], on_line(0, -1)),
            remote(zs.at[half, 0], zr.at[half, 0], ss.at[half, 4], rs.at[half, 4], on_line(1)),
            remote(zs.at[half, 1], zr.at[half, 1], ss.at[half, 5], rs.at[half, 5], on_line(-1)),
        ]
        for c in out:
            c.start()
        return out

    def relay(half):
        side = jnp.where(top, 0, 1)
        return remote(xr.at[half, 2], xr.at[half, side], ss.at[half, 6], rs.at[half, side],
                      either(top, at(half_way, 0), at(-half_way, low_n - 1)))

    def pass_on(half):
        @pl.when(top | bottom)
        def _():
            remote(xr.at[half, 2], xr.at[half, 2], ss.at[half, 6], rs.at[half, 6], on_line(1)).wait_recv()
            relay(half).start()

    def wait_face(half, i):
        dst = (xr.at[half, 0], xr.at[half, 1], yr.at[half, 0], yr.at[half, 1], zr.at[half, 0], zr.at[half, 1])[i]
        remote(dst, dst, ss.at[half, i], rs.at[half, i], on_line(1)).wait_recv()

    edge = top | bottom
    side = jnp.where(top, half_way, -half_way)
    to_relay = on_line(side)
    telling = [
        remote(pk.at[pl.ds(0, 5)], mk.at[pl.ds(3, 5)], ss.at[4, 0], rs.at[4, 0], to_relay),
        remote(pk.at[pl.ds(5, 5)], mk.at[pl.ds(8, 5)], ss.at[4, 1], rs.at[4, 1], to_relay),
        remote(u.at[0, jnp.where(top, 1, 0)], mu, ss.at[4, 2], rs.at[4, 2],
               at(side, jnp.where(top, 0, low_n - 1))),
        remote(pk.at[pl.ds(10, 1)], mk.at[pl.ds(13, 1)], ss.at[4, 3], rs.at[4, 3], to_relay),
    ]
    first = at(side, jnp.where(top, 0, low_n - 1))
    second = at(side, jnp.where(top, 1, low_n - 2))
    slot_first, slot_second = jnp.where(top, 0, 1), jnp.where(top, 2, 3)

    def pass_layer(k, frm, count, to, sem, dev):
        return remote(mk.at[pl.ds(frm, count)], e.at[pl.ds(to, count)], ss.at[5, k], rs.at[2, sem], dev)

    passing = [
        pass_layer(0, 16, 1, jnp.where(top, 3, 6), slot_first, first),
        pass_layer(1, 16, 1, jnp.where(top, 1, 8), slot_second, second),
        pass_layer(2, 13, 1, jnp.where(top, 2, 7), slot_first, first),
        pass_layer(3, 13, 1, jnp.where(top, 0, 9), slot_second, second),
        pass_layer(4, 14, 2, jnp.where(top, 0, 8), slot_second, first),
    ]

    zero = jnp.zeros((8, 128), F32)
    loads[0].wait()
    loads[1].wait()
    hold(0, disp)
    loads[3].wait()
    loads[4].wait()
    for c in range(3):
        pk[c] = jnp.where(top, u[0, 0, c], u[0, 1, c])
    pk[3] = jnp.where(top, emax[1], emax[0])
    pk[4] = jnp.where(top, reg[1], reg[0]).astype(F32)
    pl.semaphore_wait(barrier, len(greet))
    faces = [send_faces(0)]

    @pl.when(edge)
    def _():
        telling[2].start()
        telling[0].start()


    steps = []
    reach = 1
    while reach < line_n // 2:
        steps.append(reach)
        reach *= 2

    def dbl_signal(s):
        if s < len(steps):
            signal(dbl.at[s], on_line(steps[s]))
            signal(dbl.at[s], on_line(-steps[s]))

    known = set()

    def dbl_wait(s):
        if s < len(steps) and s not in known:
            known.add(s)
            pl.semaphore_wait(dbl.at[s], 2)

    dbl_signal(0)
    loads[2].wait()
    for c in loads[5:10]:
        c.wait()
    hold(1, dold)
    faces.append(send_faces(1))
    dbl_wait(0)
    dbl_signal(1)

    def pick(table, where_is):
        out = table[REGIONS - 1]
        for k in range(REGIONS - 2, -1, -1):
            out = jnp.where(where_is[k], table[k], out)
        return out

    is_region = [[reg[l] == k for k in range(REGIONS)] for l in range(2)]
    shear_c = [pick([shear[k] for k in range(REGIONS)], is_region[l]) for l in range(2)]
    ratio_c = [pick([ratio[k] for k in range(REGIONS)], is_region[l]) for l in range(2)]
    scale_c = [pick([scale[k] for k in range(REGIONS)], is_region[l]) for l in range(2)]

    def flats(half):
        from_lo = zr[half, 0] * zlo_on
        from_hi = zr[half, 1] * zhi_on
        out = []
        for l in range(2):
            grad_y, grad_z = [], []
            for c in range(3):
                j = l * 3 + c
                val = u[half, l, c]
                below = jnp.broadcast_to(yr[half, 0, j] * ylo_on, (8, 128))
                above = jnp.broadcast_to(yr[half, 1, j] * yhi_on, (8, 128))
                prev_y = pltpu.roll(jnp.where(row == 7, below, val), 1, 0)
                next_y = pltpu.roll(jnp.where(row == 0, above, val), 7, 0)
                prev_z = jnp.where(lane == 0, pltpu.roll(from_lo, (128 - j) % 128, 1), pltpu.roll(val, 1, 1))
                next_z = jnp.where(lane == 127, pltpu.roll(from_hi, 127 - j, 1), pltpu.roll(val, 127, 1))
                grad_y.append(0.5 * (next_y - prev_y))
                grad_z.append(0.5 * (next_z - prev_z))
            out.append(flat_parts(grad_y, grad_z))
        return out

    def strains(half, flat):
        out = []
        for l in range(2):
            grad_x = []
            for c in range(3):
                prev_x = xr[half, 0, c] if l == 0 else u[half, 0, c]
                next_x = xr[half, 1, c] if l == 1 else u[half, 1, c]
                grad_x.append(0.5 * (next_x - prev_x))
            out.append(deviator(grad_x, flat[l]))
        return out

    def drive_of(d, g, r, m, most):
        energy = g * (
            d[0] * d[0] + d[1] * d[1] + d[2] * d[2] + 2.0 * (d[3] * d[3] + d[4] * d[4] + d[5] * d[5]))
        peak = jnp.maximum(most, energy)
        soft = 1.0 - lax.erf((peak - energy) / m) / r
        return peak, soft, soft * energy

    for i in range(2, 6):
        wait_face(0, i)
    flat_new = flats(0)
    for i in range(5):
        pk[5 + i] = jnp.where(top, flat_new[1][i], flat_new[0][i])

    @pl.when(edge)
    def _():
        telling[1].start()

    @pl.when(jnp.logical_not(bottom))
    def _():
        wait_face(0, 0)

    @pl.when(jnp.logical_not(top))
    def _():
        wait_face(0, 1)

    @pl.when(edge)
    def _():
        near = [xr[0, jnp.where(top, 0, 1), c] for c in range(3)]
        grad_x = [0.5 * (jnp.where(top, u[0, 1, c], near[c]) - jnp.where(top, near[c], u[0, 0, c]))
                  for c in range(3)]
        flat = [jnp.where(top, flat_new[0][i], flat_new[1][i]) for i in range(5)]
        both = [jnp.where(top, a, b) for a, b in (
            (shear_c[0], shear_c[1]), (ratio_c[0], ratio_c[1]), (scale_c[0], scale_c[1]), (emax[0], emax[1]))]
        pk[10] = drive_of(deviator(grad_x, flat), *both)[2]
        telling[3].start()

    dbl_wait(1)
    dbl_signal(2)
    pass_on(0)

    @pl.when(edge)
    def _():
        for c in telling[:3]:
            c.wait_recv()
        grad_x = [0.5 * (jnp.where(top, mu[c], mk[3 + c]) - jnp.where(top, mk[3 + c], mu[c])) for c in range(3)]
        theirs = [mk[7] == float(k) for k in range(REGIONS)]
        both = [pick([t[k] for k in range(REGIONS)], theirs) for t in (shear, ratio, scale)]
        mk[16] = drive_of(deviator(grad_x, [mk[8 + i] for i in range(5)]), *both, mk[6])[2]
        passing[0].start()
        passing[1].start()
        telling[3].wait_recv()
        passing[2].start()
        passing[3].start()
        remote(mk.at[pl.ds(14, 2)], mk.at[pl.ds(14, 2)], ss.at[4, 4], rs.at[4, 4], to_relay).wait_recv()
        passing[4].start()

    pass_on(1)

    @pl.when(bottom)
    def _():
        wait_face(0, 0)

    @pl.when(top)
    def _():
        wait_face(0, 1)

    dev_new = strains(0, flat_new)
    softening = []
    for l in range(2):
        enext[l], soft, e[4 + l] = drive_of(dev_new[l], shear_c[l], ratio_c[l], scale_c[l], emax[l])
        softening.append(soft)

    own = e.at[pl.ds(4, 2)]
    wide = [
        remote(own, e.at[pl.ds(2, 2)], ss.at[2, 0], rs.at[2, 0], on_x(1)),
        remote(own, e.at[pl.ds(6, 2)], ss.at[2, 1], rs.at[2, 1], on_x(-1)),
        remote(own, e.at[pl.ds(0, 2)], ss.at[2, 2], rs.at[2, 2], on_x(2)),
        remote(own, e.at[pl.ds(8, 2)], ss.at[2, 3], rs.at[2, 3], on_x(-2)),
    ]
    under, above_ = low == low_n - 2, low == 1
    spread = list(zip((jnp.logical_not(top), jnp.logical_not(bottom), low < low_n - 2, low > 1), wide))
    spread.append((under | above_, remote(
        own, mk.at[pl.ds(14, 2)], ss.at[4, 4], rs.at[4, 4],
        at(jnp.where(under, half_way, -half_way), jnp.where(under, low_n - 1, 0)))))
    for cond, c in reversed(spread):
        pl.when(cond)(c.start)
    dbl_wait(2)
    dbl_signal(3)

    row_mask = jnp.where(row < 4, yhi_on, ylo_on)
    lane_mask = jnp.where(lane < 4, zhi_on, jnp.where(lane >= 124, zlo_on, 0.0))
    masks = {(1, 0): row_mask, (0, 1): lane_mask, (1, 1): row_mask * lane_mask}
    to_hi, to_lo = zero, zero
    basis = {}
    for l in (4, 5, 2, 3, 6, 7, 0, 1, 8, 9):
        if l in (2, 6, 0, 8):
            wide[(2, 6, 0, 8).index(l)].wait_recv()
        val = e[l]
        basis[(l, 0, 0)] = val
        if 1 <= l <= 8:
            j = l - 1
            eys[0, j] = val[4:8]
            eys[1, j] = val[0:4]
            here = (lane >= 4 * j) & (lane < 4 * j + 4)
            to_hi = jnp.where(here, pltpu.roll(val, (4 * j - 124) % 128, 1), to_hi)
            to_lo = jnp.where(here, pltpu.roll(val, 4 * j, 1) if j else val, to_lo)
    ezs[0] = to_hi
    ezs[1] = to_lo
    edges = [
        remote(ezs.at[0], ezr.at[2], ss.at[3, 0], rs.at[3, 0], on_line(1, 1)),
        remote(ezs.at[0], ezr.at[3], ss.at[3, 1], rs.at[3, 1], on_line(1, -1)),
        remote(ezs.at[1], ezr.at[4], ss.at[3, 2], rs.at[3, 2], on_line(-1, 1)),
        remote(ezs.at[1], ezr.at[5], ss.at[3, 3], rs.at[3, 3], on_line(-1, -1)),
        remote(ezs.at[0], ezr.at[0], ss.at[3, 4], rs.at[3, 4], on_line(1)),
        remote(ezs.at[1], ezr.at[1], ss.at[3, 5], rs.at[3, 5], on_line(-1)),
        remote(eys.at[0], eyr.at[0], ss.at[3, 6], rs.at[3, 6], on_line(0, 1)),
        remote(eys.at[1], eyr.at[1], ss.at[3, 7], rs.at[3, 7], on_line(0, -1)),
    ]
    for c in edges:
        c.start()
    for c in edges[6:]:
        c.wait_recv()
    for l in range(1, 9):
        basis[(l, 1, 0)] = jnp.concatenate([eyr[1, l - 1], eyr[0, l - 1]], axis=0) * row_mask
    for c in edges[:6]:
        c.wait_recv()
    sides = ((ezr[0], ezr[1]),
             (jnp.where(row < 4, ezr[3], ezr[2]), jnp.where(row < 4, ezr[5], ezr[4])))
    for l in range(1, 9):
        for t in range(2):
            j = l - 1
            from_lo, from_hi = sides[t]
            val = jnp.where(lane < 4,
                            pltpu.roll(from_hi, 128 - 4 * j, 1) if j else from_hi,
                            pltpu.roll(from_lo, 124 - 4 * j, 1))
            basis[(l, t, 1)] = val * masks[(t, 1)]

    def grow(now, k):
        cache = {}

        def rolled(key, amount, axis):
            at = (key, amount, axis)
            if at not in cache:
                cache[at] = pltpu.roll(now[key], amount, axis)
            return cache[at]

        out = {}
        for l in range(k + 1, 9 - k):
            inner = k + 2 <= l <= 7 - k
            for ty, tz in ((0, 0), (1, 0), (0, 1), (1, 1)) if inner else ((0, 0),):
                me = (l, ty, tz)
                acc = now[(l - 1, ty, tz)] + now[(l + 1, ty, tz)]
                acc = acc + jnp.where(row == 7, rolled((l, 1 - ty, tz), 7, 0), rolled(me, 7, 0))
                acc = acc + jnp.where(row == 0, rolled((l, 1 - ty, tz), 1, 0), rolled(me, 1, 0))
                acc = acc + jnp.where(lane == 127, rolled((l, ty, 1 - tz), 127, 1), rolled(me, 127, 1))
                acc = acc + jnp.where(lane == 0, rolled((l, ty, 1 - tz), 1, 1), rolled(me, 1, 1))
                acc = acc * (1.0 / 6.0)
                acc = now[me] - acc if SHIFTS[k] == 1.0 else -acc
                if (ty, tz) != (0, 0):
                    acc = acc * masks[(ty, tz)]
                out[me] = acc
        return out

    powers = [basis]
    for k in range(ITERS):
        powers.append(grow(powers[-1], k))
    vecs = [[p[(4, 0, 0)], p[(5, 0, 0)]] for p in powers]

    for k in range(ITERS + 1):
        for l in range(2):
            vout[2 * k + l] = vecs[k][l]
    sums = zero
    for n, (i, j) in enumerate(PAIRS):
        part = vecs[i][0] * vecs[j][0] + vecs[i][1] * vecs[j][1]
        sums = jnp.where(lane == n, jnp.sum(part, axis=1, keepdims=True), sums)
    mine = jnp.sum(sums, axis=0, keepdims=True)

    gs[0] = mine
    sends = []
    for d in range(1, plane_n):
        c = remote(gs.at[0], gp.at[d - 1], ps_sem, pr_sem, on_plane(d))
        c.start()
    every = remote(gp, gp, ps_sem, pr_sem, on_plane(1))
    every.wait_recv()
    acc = mine
    for d in range(plane_n - 1):
        acc = acc + gp[d]
    ts[0] = acc
    dbl_wait(len(steps) - 1)
    order = sorted(range(1, line_n), key=lambda d: -min(d, line_n - d))
    for d in order:
        c = remote(ts.at[0], tr.at[d - 1], ls_sem, lr_sem, on_line(d))
        c.start()
    for i in range(6):
        wait_face(1, i)
    loads[10].wait()
    dev_old = strains(1, flats(1))
    jump = [[2.0 * shear_c[l] * (dev_new[l][a] - dev_old[l][a]) for a in range(6)] for l in range(2)]
    total = [[None] * 6 for _ in range(2)]
    for k in range(TERMS):
        for l in range(2):
            tau = pick([times[r, k] for r in range(REGIONS)], is_region[l])
            mod = pick([moduli[r, k] for r in range(REGIONS)], is_region[l])
            decay = jnp.exp(-1.0 / tau)
            weight = mod * (1.0 - decay) * tau
            for a in range(6):
                val = decay * visc[k, a, l] + weight * jump[l][a]
                vnext[k, a, l] = val
                total[l][a] = val if k == 0 else total[l][a] + val
    for l in range(2):
        sums = []
        for r in range(REGIONS):
            s = moduli[r, 0]
            for k in range(1, TERMS):
                s = s + moduli[r, k]
            sums.append(1.0 - s)
        factor = pick(sums, is_region[l]) * 2.0 * shear_c[l]
        for a in range(6):
            stress[a, l] = softening[l] * (factor * dev_new[l][a] + total[l][a])

    along = remote(tr, tr, ls_sem, lr_sem, on_line(1))
    along.wait_recv()
    for d in range(line_n - 1):
        acc = acc + tr[d]
    sums_out[...] = acc

    for group in (faces[0], faces[1], edges):
        for c in group:
            c.wait_send()

    for cond, c in spread:
        pl.when(cond)(c.wait_send)

    @pl.when(edge)
    def _():
        relay(0).wait_send()
        relay(1).wait_send()
        for c in telling + passing:
            c.wait_send()

    every.wait_send()
    along.wait_send()


def finish(stress, vnext, enext, vecs, sums, stress_h, vnext_h, enext_h, field_h, resid_h, field, resid, sem):
    stores = [pltpu.make_async_copy(a, b, sem.at[i]) for i, (a, b) in enumerate(
        ((vnext, vnext_h), (stress, stress_h), (enext, enext_h), (field, field_h), (resid, resid_h)))]
    for c in stores[:3]:
        c.start()
    full = jnp.broadcast_to(sums[...], (8, 128))
    gram = {pair: jnp.broadcast_to(full[:, n:n + 1], (8, 128)) for n, pair in enumerate(PAIRS)}
    on_field, on_resid = coefficients(gram)
    for l in range(2):
        val = on_field[0] * vecs[l]
        for k in range(1, ITERS):
            val = val + on_field[k] * vecs[2 * k + l]
        field[l] = val
        val = on_resid[0] * vecs[l]
        for k in range(1, ITERS + 1):
            val = val + on_resid[k] * vecs[2 * k + l]
        resid[l] = val
    for c in stores[3:]:
        c.start()
    for c in stores:
        c.wait()


def solution(mesh):
    nx, ny, nz = mesh.shape["gx"], mesh.shape["gy"], mesh.shape["gz"]
    zhi = 4 if nx % 32 == 0 else 2
    low_n = nx // zhi
    line_n, plane_n = zhi * nz, low_n * ny

    def on_device(*args):
        hbm = pl.BlockSpec(memory_space=pltpu.HBM)
        local = pl.BlockSpec(memory_space=pltpu.VMEM)
        vm = pltpu.VMEM
        sm = pltpu.SMEM
        dma = pltpu.SemaphoreType.DMA
        cells = jax.ShapeDtypeStruct((2, 8, 128), F32)
        stress = jax.ShapeDtypeStruct((6, 2, 8, 128), F32)
        visco = jax.ShapeDtypeStruct((6, 6, 2, 8, 128), F32)
        parts = pl.pallas_call(
            functools.partial(kernel, (nx, ny, nz, zhi)),
            out_shape=(stress, visco, cells,
                       jax.ShapeDtypeStruct((10, 8, 128), F32), jax.ShapeDtypeStruct((1, 128), F32)),
            in_specs=[hbm] * 11,
            out_specs=[local] * 5,
            scratch_shapes=[
                vm((3, 2, 8, 128), F32), vm((3, 2, 8, 128), F32), vm((6, 6, 2, 8, 128), F32),
                vm((2, 8, 128), F32), vm((2, 8, 128), jnp.int32), vm((2, 8, 128), jnp.int32),
                sm((4, 6), F32), sm((4, 6), F32), sm((4,), F32), sm((4,), F32), sm((4,), F32),
                vm((2, 2, 3, 8, 128), F32), vm((2, 3, 3, 8, 128), F32),
                vm((2, 2, 6, 1, 128), F32), vm((2, 2, 6, 1, 128), F32),
                vm((2, 2, 8, 128), F32), vm((2, 2, 8, 128), F32),
                vm((10, 8, 128), F32),
                vm((2, 8, 4, 128), F32), vm((2, 8, 4, 128), F32),
                vm((2, 8, 128), F32), vm((6, 8, 128), F32),
                vm((1, 1, 128), F32), vm((plane_n - 1, 1, 128), F32),
                vm((1, 1, 128), F32), vm((line_n - 1, 1, 128), F32),
                vm((11, 8, 128), F32), vm((17, 8, 128), F32), vm((3, 8, 128), F32),
                dma((11,)), dma((6, 8)), dma((6, 8)), dma, dma, dma, dma,
                pltpu.SemaphoreType.REGULAR((4,)),
            ],
            compiler_params=pltpu.CompilerParams(
                collective_id=0, has_side_effects=True, vmem_limit_bytes=16 << 20),
        )(*[pltpu.with_memory_space_constraint(a, pltpu.HBM) for a in args])
        return pl.pallas_call(
            finish,
            out_shape=(stress, visco, cells, cells, cells),
            in_specs=[local] * 5,
            out_specs=[hbm] * 5,
            scratch_shapes=[vm((2, 8, 128), F32), vm((2, 8, 128), F32), dma((5,))],
            compiler_params=pltpu.CompilerParams(vmem_limit_bytes=16 << 20),
        )(*parts)

    cell = P("gx", "gy", "gz")
    vec = P(None, "gx", "gy", "gz")
    ten = P(None, None, "gx", "gy", "gz")
    return jax.shard_map(
        on_device,
        mesh=mesh,
        in_specs=(vec, vec, ten, cell, cell, cell, P(), P(), P(), P(), P()),
        out_specs=(vec, ten, cell, cell, cell),
        check_vma=False,
    )
```

```python
import functools

import jax
import jax.numpy as jnp
from jax import lax
from jax.experimental import pallas as pl
from jax.experimental.pallas import tpu as pltpu
from jax.sharding import PartitionSpec as P

ITERS = 4
TERMS = 6
REGIONS = 4
SHIFTS = (1.0, 25.0, 25.0, 1.0)
PAIRS = tuple((i, j) for i in range(4) for j in range(i, 5))
F32 = jnp.float32


def flat_parts(grad_y, grad_z):
    return (grad_y[1], grad_z[2], 0.5 * (grad_z[1] + grad_y[2]), grad_z[0], grad_y[0])


def deviator(grad_x, flat):
    xx, yy, zz = grad_x[0], flat[0], flat[1]
    third = (xx + yy + zz) * (1.0 / 3.0)
    return (
        xx - third,
        yy - third,
        zz - third,
        flat[2],
        0.5 * (flat[3] + grad_x[2]),
        0.5 * (flat[4] + grad_x[1]),
    )


def coefficients(gram):
    def form(left, right):
        total = None
        for i, a in enumerate(left):
            row = None
            for j, b in enumerate(right):
                term = b * gram[(min(i, j), max(i, j))]
                row = term if row is None else row + term
            row = a * row
            total = row if total is None else total + row
        return total

    one = jnp.ones_like(gram[(0, 0)])
    res, direction, field = [one], [one], []
    norm = gram[(0, 0)]
    for step in range(ITERS):
        image = []
        for k in range(step + 2):
            value = None
            if k <= step:
                value = SHIFTS[k] * direction[k]
            if k >= 1:
                value = 24.0 * direction[k - 1] if value is None else value + 24.0 * direction[k - 1]
            image.append(value)
        alpha = norm / form(direction, image)
        field = [field[k] + alpha * direction[k] if k < step else alpha * direction[k] for k in range(step + 1)]
        res = [res[k] - alpha * image[k] if k <= step else -alpha * image[k] for k in range(step + 2)]
        if step + 1 < ITERS:
            new = form(res, res)
            beta = new / norm
            direction = [res[k] + beta * direction[k] if k <= step else res[k] for k in range(step + 2)]
            norm = new
    return field, res


def kernel(sizes, *refs):
    nx, ny, nz, zhi = sizes
    low_n = nx // zhi
    line_n = zhi * nz
    plane_n = low_n * ny
    half_way = nz // 2
    (disp_h, dold_h, visc_h, emax_h, reg_h, dir_h, moduli_h, times_h, shear_h, ratio_h, scale_h,
     stress, vnext, enext, vout, sums_out,
     disp, dold, visc, emax, reg, dirm, moduli, times, shear, ratio, scale,
     u, xr, ys, yr, zs, zr, e, eys, eyr, ezs, ezr, gs, gp, ts, tr,
     pk, mk, mu, ld_sem, ss, rs, ps_sem, pr_sem, ls_sem, lr_sem, dbl) = refs

    ix, iy, iz = lax.axis_index("gx"), lax.axis_index("gy"), lax.axis_index("gz")
    low, hi = lax.rem(ix, low_n), lax.div(ix, low_n)
    spot = hi * nz + iz
    place = low * ny + iy
    top = low == low_n - 1
    bottom = low == 0

    def wrap(q, n):
        return jnp.where(q >= n, q - n, q)

    def on_x(d):
        return {"gx": wrap(ix + d % nx, nx), "gy": iy, "gz": iz}

    def at(d, low_to, dy=0):
        q = wrap(spot + (d % line_n if isinstance(d, int) else d), line_n)
        y_to = wrap(iy + dy % ny, ny) if dy else iy
        return {"gx": lax.div(q, nz) * low_n + low_to, "gy": y_to, "gz": lax.rem(q, nz)}

    def on_line(d, dy=0):
        return at(d, low, dy)

    def on_plane(d):
        q = wrap(place + d, plane_n)
        return {"gx": hi * low_n + lax.div(q, ny), "gy": lax.rem(q, ny), "gz": iz}

    def either(cond, one, other):
        return {k: jnp.where(cond, one[k], other[k]) for k in one}

    def signal(sem, dev):
        pl.semaphore_signal(sem, inc=1, device_id=dev, device_id_type=pl.DeviceIdType.MESH)

    def remote(src, dst, ssem, rsem, dev):
        return pltpu.make_async_remote_copy(
            src_ref=src, dst_ref=dst, send_sem=ssem, recv_sem=rsem,
            device_id=dev, device_id_type=pl.DeviceIdType.MESH)

    loads = [pltpu.make_async_copy(a, b, ld_sem.at[i]) for i, a, b in (
        (0, dir_h, dirm), (1, disp_h, disp), (4, dold_h, dold), (2, reg_h, reg), (3, emax_h, emax),
        (0, shear_h, shear), (1, ratio_h, ratio), (2, scale_h, scale), (3, moduli_h, moduli), (5, times_h, times),
        (4, visc_h, visc))]
    for c in loads[:2]:
        c.start()

    barrier = pltpu.get_barrier_semaphore()
    greet = [at(s, wrap(low + r % low_n, low_n)) for r in (0, 1, -1, 2, -2) for s in (half_way, -half_way)]
    greet += [on_plane(d) for d in range(1, plane_n)]
    greet += [on_line(1), on_line(-1)]
    for dev in greet:
        signal(barrier, dev)
    for c in loads[2:5]:
        c.start()

    row = lax.broadcasted_iota(jnp.int32, (8, 128), 0)
    lane = lax.broadcasted_iota(jnp.int32, (8, 128), 1)
    ylo_on = jnp.where(iy > 0, 1.0, 0.0).astype(F32)
    yhi_on = jnp.where(iy < ny - 1, 1.0, 0.0).astype(F32)
    zlo_on = jnp.where(iz > 0, 1.0, 0.0).astype(F32)
    zhi_on = jnp.where(iz < nz - 1, 1.0, 0.0).astype(F32)

    def hold(half, src):
        to_hi, to_lo = zero, zero
        for l in range(2):
            free = (1 - dirm[l]).astype(F32)
            for c in range(3):
                j = l * 3 + c
                val = src[c, l] * free
                u[half, l, c] = val
                ys[half, 0, j] = val[7:8]
                ys[half, 1, j] = val[0:1]
                to_hi = jnp.where(lane == j, pltpu.roll(val, (j - 127) % 128, 1), to_hi)
                to_lo = jnp.where(lane == j, pltpu.roll(val, j, 1) if j else val, to_lo)
        zs[half, 0] = to_hi
        zs[half, 1] = to_lo

    def send_faces(half):
        out = [
            remote(u.at[half, 1], xr.at[half, jnp.where(top, 2, 0)], ss.at[0],
                   rs.at[7 * half + jnp.where(top, 6, 0)], either(top, on_line(half_way), on_x(1))),
            remote(u.at[half, 0], xr.at[half, jnp.where(bottom, 2, 1)], ss.at[1],
                   rs.at[7 * half + jnp.where(bottom, 6, 1)], either(bottom, on_line(-half_way), on_x(-1))),
            remote(ys.at[half, 0], yr.at[half, 0], ss.at[2], rs.at[7 * half + 2], on_line(0, 1)),
            remote(ys.at[half, 1], yr.at[half, 1], ss.at[3], rs.at[7 * half + 3], on_line(0, -1)),
            remote(zs.at[half, 0], zr.at[half, 0], ss.at[4], rs.at[7 * half + 4], on_line(1)),
            remote(zs.at[half, 1], zr.at[half, 1], ss.at[5], rs.at[7 * half + 5], on_line(-1)),
        ]
        for c in out:
            c.start()
        return out

    def relay(half):
        side = jnp.where(top, 0, 1)
        return remote(xr.at[half, 2], xr.at[half, side], ss.at[6], rs.at[7 * half + side],
                      either(top, at(half_way, 0), at(-half_way, low_n - 1)))

    def pass_on(half):
        @pl.when(top | bottom)
        def _():
            remote(xr.at[half, 2], xr.at[half, 2], ss.at[6], rs.at[7 * half + 6], on_line(1)).wait_recv()
            relay(half).start()

    def wait_face(half, i):
        dst = (xr.at[half, 0], xr.at[half, 1], yr.at[half, 0], yr.at[half, 1], zr.at[half, 0], zr.at[half, 1])[i]
        remote(dst, dst, ss.at[i], rs.at[7 * half + i], on_line(1)).wait_recv()

    edge = top | bottom
    side = jnp.where(top, half_way, line_n - half_way)
    to_relay = on_line(side)
    telling = [
        remote(pk.at[pl.ds(0, 5)], mk.at[pl.ds(3, 5)], ss.at[11 + 0], rs.at[26 + 0], to_relay),
        remote(pk.at[pl.ds(5, 5)], mk.at[pl.ds(8, 5)], ss.at[11 + 1], rs.at[26 + 1], to_relay),
        remote(u.at[0, jnp.where(top, 1, 0)], mu, ss.at[11 + 2], rs.at[26 + 2],
               at(side, jnp.where(top, 0, low_n - 1))),
        remote(pk.at[pl.ds(10, 1)], mk.at[pl.ds(13, 1)], ss.at[11 + 3], rs.at[26 + 3], to_relay),
    ]
    first = at(side, jnp.where(top, 0, low_n - 1))
    second = at(side, jnp.where(top, 1, low_n - 2))
    slot_first, slot_second = jnp.where(top, 0, 1), jnp.where(top, 2, 3)

    def pass_layer(k, frm, count, to, sem, dev):
        return remote(mk.at[pl.ds(frm, count)], e.at[pl.ds(to, count)], ss.at[16 + k], rs.at[14 + sem], dev)

    passing = [
        pass_layer(0, 16, 1, jnp.where(top, 3, 6), slot_first, first),
        pass_layer(1, 16, 1, jnp.where(top, 1, 8), slot_second, second),
        pass_layer(2, 13, 1, jnp.where(top, 2, 7), slot_first, first),
        pass_layer(3, 13, 1, jnp.where(top, 0, 9), slot_second, second),
        pass_layer(4, 14, 2, jnp.where(top, 0, 8), slot_second, first),
    ]

    zero = jnp.zeros((8, 128), F32)
    loads[0].wait()
    loads[1].wait()
    hold(0, disp)
    loads[3].wait()
    loads[4].wait()
    for c in range(3):
        pk[c] = jnp.where(top, u[0, 0, c], u[0, 1, c])
    pk[3] = jnp.where(top, emax[1], emax[0])
    pk[4] = jnp.where(top, reg[1], reg[0]).astype(F32)
    pl.semaphore_wait(barrier, len(greet))
    faces = [send_faces(0)]

    @pl.when(edge)
    def _():
        telling[2].start()
        telling[0].start()

    for c in loads[5:10]:
        c.start()

    steps = []
    reach = 1
    while reach < line_n // 2:
        steps.append(reach)
        reach *= 2

    def dbl_signal(s):
        if s < len(steps):
            signal(dbl.at[s], on_line(steps[s]))
            signal(dbl.at[s], on_line(-steps[s]))

    known = set()

    def dbl_wait(s):
        if s < len(steps) and s not in known:
            known.add(s)
            pl.semaphore_wait(dbl.at[s], 2)

    dbl_signal(0)
    loads[2].wait()
    hold(1, dold)
    loads[10].start()
    for c in loads[5:10]:
        c.wait()
    dbl_wait(0)
    dbl_signal(1)

    def pick(table, where_is):
        out = table[REGIONS - 1]
        for k in range(REGIONS - 2, -1, -1):
            out = jnp.where(where_is[k], table[k], out)
        return out

    is_region = [[reg[l] == k for k in range(REGIONS)] for l in range(2)]
    shear_c = [pick([shear[k] for k in range(REGIONS)], is_region[l]) for l in range(2)]
    ratio_c = [pick([ratio[k] for k in range(REGIONS)], is_region[l]) for l in range(2)]
    scale_c = [pick([scale[k] for k in range(REGIONS)], is_region[l]) for l in range(2)]

    def flats(half):
        from_lo = zr[half, 0] * zlo_on
        from_hi = zr[half, 1] * zhi_on
        out = []
        for l in range(2):
            grad_y, grad_z = [], []
            for c in range(3):
                j = l * 3 + c
                val = u[half, l, c]
                below = jnp.broadcast_to(yr[half, 0, j] * ylo_on, (8, 128))
                above = jnp.broadcast_to(yr[half, 1, j] * yhi_on, (8, 128))
                prev_y = pltpu.roll(jnp.where(row == 7, below, val), 1, 0)
                next_y = pltpu.roll(jnp.where(row == 0, above, val), 7, 0)
                prev_z = jnp.where(lane == 0, pltpu.roll(from_lo, (128 - j) % 128, 1), pltpu.roll(val, 1, 1))
                next_z = jnp.where(lane == 127, pltpu.roll(from_hi, 127 - j, 1), pltpu.roll(val, 127, 1))
                grad_y.append(0.5 * (next_y - prev_y))
                grad_z.append(0.5 * (next_z - prev_z))
            out.append(flat_parts(grad_y, grad_z))
        return out

    def strains(half, flat):
        out = []
        for l in range(2):
            grad_x = []
            for c in range(3):
                prev_x = xr[half, 0, c] if l == 0 else u[half, 0, c]
                next_x = xr[half, 1, c] if l == 1 else u[half, 1, c]
                grad_x.append(0.5 * (next_x - prev_x))
            out.append(deviator(grad_x, flat[l]))
        return out

    def drive_of(d, g, r, m, most):
        energy = g * (
            d[0] * d[0] + d[1] * d[1] + d[2] * d[2] + 2.0 * (d[3] * d[3] + d[4] * d[4] + d[5] * d[5]))
        peak = jnp.maximum(most, energy)
        soft = 1.0 - lax.erf((peak - energy) / m) / r
        return peak, soft, soft * energy

    for i in range(2, 6):
        wait_face(0, i)
    flat_new = flats(0)
    for i in range(5):
        pk[5 + i] = jnp.where(top, flat_new[1][i], flat_new[0][i])

    @pl.when(edge)
    def _():
        telling[1].start()

    @pl.when(jnp.logical_not(bottom))
    def _():
        wait_face(0, 0)

    @pl.when(jnp.logical_not(top))
    def _():
        wait_face(0, 1)

    @pl.when(edge)
    def _():
        near = [xr[0, jnp.where(top, 0, 1), c] for c in range(3)]
        grad_x = [0.5 * (jnp.where(top, u[0, 1, c], near[c]) - jnp.where(top, near[c], u[0, 0, c]))
                  for c in range(3)]
        flat = [jnp.where(top, flat_new[0][i], flat_new[1][i]) for i in range(5)]
        both = [jnp.where(top, a, b) for a, b in (
            (shear_c[0], shear_c[1]), (ratio_c[0], ratio_c[1]), (scale_c[0], scale_c[1]), (emax[0], emax[1]))]
        pk[10] = drive_of(deviator(grad_x, flat), *both)[2]
        telling[3].start()

    dbl_wait(1)
    dbl_signal(2)
    pass_on(0)

    @pl.when(edge)
    def _():
        for c in telling[:3]:
            c.wait_recv()
        grad_x = [0.5 * (jnp.where(top, mu[c], mk[3 + c]) - jnp.where(top, mk[3 + c], mu[c])) for c in range(3)]
        theirs = [mk[7] == float(k) for k in range(REGIONS)]
        both = [pick([t[k] for k in range(REGIONS)], theirs) for t in (shear, ratio, scale)]
        mk[16] = drive_of(deviator(grad_x, [mk[8 + i] for i in range(5)]), *both, mk[6])[2]
        passing[0].start()
        passing[1].start()
        telling[3].wait_recv()
        passing[2].start()
        passing[3].start()
        remote(mk.at[pl.ds(14, 2)], mk.at[pl.ds(14, 2)], ss.at[11 + 4], rs.at[26 + 4], to_relay).wait_recv()
        passing[4].start()

    @pl.when(bottom)
    def _():
        wait_face(0, 0)

    @pl.when(top)
    def _():
        wait_face(0, 1)

    dev_new = strains(0, flat_new)
    softening = []
    for l in range(2):
        enext[l], soft, e[4 + l] = drive_of(dev_new[l], shear_c[l], ratio_c[l], scale_c[l], emax[l])
        softening.append(soft)

    own = e.at[pl.ds(4, 2)]
    wide = [
        remote(own, e.at[pl.ds(2, 2)], ss.at[7 + 0], rs.at[14 + 0], on_x(1)),
        remote(own, e.at[pl.ds(6, 2)], ss.at[7 + 1], rs.at[14 + 1], on_x(-1)),
        remote(own, e.at[pl.ds(0, 2)], ss.at[7 + 2], rs.at[14 + 2], on_x(2)),
        remote(own, e.at[pl.ds(8, 2)], ss.at[7 + 3], rs.at[14 + 3], on_x(-2)),
    ]
    under, above_ = low == low_n - 2, low == 1
    spread = list(zip((jnp.logical_not(top), jnp.logical_not(bottom), low < low_n - 2, low > 1), wide))
    spread.append((under | above_, remote(
        own, mk.at[pl.ds(14, 2)], ss.at[11 + 4], rs.at[26 + 4],
        at(jnp.where(under, half_way, line_n - half_way), jnp.where(under, low_n - 1, 0)))))
    for cond, c in reversed(spread):
        pl.when(cond)(c.start)
    for c in faces[0]:
        c.wait_send()
    faces.append(send_faces(1))
    dbl_wait(2)
    dbl_signal(3)

    row_mask = jnp.where(row < 4, yhi_on, ylo_on)
    lane_mask = jnp.where(lane < 4, zhi_on, jnp.where(lane >= 124, zlo_on, 0.0))
    masks = {(1, 0): row_mask, (0, 1): lane_mask, (1, 1): row_mask * lane_mask}
    to_hi, to_lo = zero, zero
    basis = {}
    for l in (4, 5, 2, 3, 6, 7, 0, 1, 8, 9):
        if l in (2, 6, 0, 8):
            wide[(2, 6, 0, 8).index(l)].wait_recv()
        val = e[l]
        basis[(l, 0, 0)] = val
        if 1 <= l <= 8:
            j = l - 1
            eys[0, j] = val[4:8]
            eys[1, j] = val[0:4]
            here = (lane >= 4 * j) & (lane < 4 * j + 4)
            to_hi = jnp.where(here, pltpu.roll(val, (4 * j - 124) % 128, 1), to_hi)
            to_lo = jnp.where(here, pltpu.roll(val, 4 * j, 1) if j else val, to_lo)
    ezs[0] = to_hi
    ezs[1] = to_lo
    edges = [
        remote(ezs.at[0], ezr.at[2], ss.at[11 + 0], rs.at[18 + 0], on_line(1, 1)),
        remote(ezs.at[0], ezr.at[3], ss.at[11 + 1], rs.at[18 + 1], on_line(1, -1)),
        remote(ezs.at[1], ezr.at[4], ss.at[11 + 2], rs.at[18 + 2], on_line(-1, 1)),
        remote(ezs.at[1], ezr.at[5], ss.at[11 + 3], rs.at[18 + 3], on_line(-1, -1)),
        remote(ezs.at[0], ezr.at[0], ss.at[11 + 4], rs.at[18 + 4], on_line(1)),
        remote(ezs.at[1], ezr.at[1], ss.at[11 + 5], rs.at[18 + 5], on_line(-1)),
        remote(eys.at[0], eyr.at[0], ss.at[11 + 6], rs.at[18 + 6], on_line(0, 1)),
        remote(eys.at[1], eyr.at[1], ss.at[11 + 7], rs.at[18 + 7], on_line(0, -1)),
    ]
    @pl.when(edge)
    def _():
        for c in telling + passing:
            c.wait_send()

    pl.when(under | above_)(spread[4][1].wait_send)
    for c in edges:
        c.start()
    for c in edges[6:]:
        c.wait_recv()
    for l in range(1, 9):
        basis[(l, 1, 0)] = jnp.concatenate([eyr[1, l - 1], eyr[0, l - 1]], axis=0) * row_mask
    for c in edges[:6]:
        c.wait_recv()
    sides = ((ezr[0], ezr[1]),
             (jnp.where(row < 4, ezr[3], ezr[2]), jnp.where(row < 4, ezr[5], ezr[4])))
    for l in range(1, 9):
        for t in range(2):
            j = l - 1
            from_lo, from_hi = sides[t]
            val = jnp.where(lane < 4,
                            pltpu.roll(from_hi, 128 - 4 * j, 1) if j else from_hi,
                            pltpu.roll(from_lo, 124 - 4 * j, 1))
            basis[(l, t, 1)] = val * masks[(t, 1)]

    def grow(now, k):
        cache = {}

        def rolled(key, amount, axis):
            at = (key, amount, axis)
            if at not in cache:
                cache[at] = pltpu.roll(now[key], amount, axis)
            return cache[at]

        out = {}
        for l in range(k + 1, 9 - k):
            inner = k + 2 <= l <= 7 - k
            for ty, tz in ((0, 0), (1, 0), (0, 1), (1, 1)) if inner else ((0, 0),):
                me = (l, ty, tz)
                acc = now[(l - 1, ty, tz)] + now[(l + 1, ty, tz)]
                acc = acc + jnp.where(row == 7, rolled((l, 1 - ty, tz), 7, 0), rolled(me, 7, 0))
                acc = acc + jnp.where(row == 0, rolled((l, 1 - ty, tz), 1, 0), rolled(me, 1, 0))
                acc = acc + jnp.where(lane == 127, rolled((l, ty, 1 - tz), 127, 1), rolled(me, 127, 1))
                acc = acc + jnp.where(lane == 0, rolled((l, ty, 1 - tz), 1, 1), rolled(me, 1, 1))
                acc = acc * (1.0 / 6.0)
                acc = now[me] - acc if SHIFTS[k] == 1.0 else -acc
                if (ty, tz) != (0, 0):
                    acc = acc * masks[(ty, tz)]
                out[me] = acc
        return out

    powers = [basis]
    for k in range(ITERS):
        powers.append(grow(powers[-1], k))
    vecs = [[p[(4, 0, 0)], p[(5, 0, 0)]] for p in powers]

    for k in range(ITERS + 1):
        for l in range(2):
            vout[2 * k + l] = vecs[k][l]
    sums = zero
    for n, (i, j) in enumerate(PAIRS):
        part = vecs[i][0] * vecs[j][0] + vecs[i][1] * vecs[j][1]
        sums = jnp.where(lane == n, jnp.sum(part, axis=1, keepdims=True), sums)
    mine = jnp.sum(sums, axis=0, keepdims=True)

    gs[0] = mine
    sends = []
    for d in range(1, plane_n):
        c = remote(gs.at[0], gp.at[d - 1], ps_sem, pr_sem, on_plane(d))
        c.start()
    every = remote(gp, gp, ps_sem, pr_sem, on_plane(1))
    pl.when(edge)(relay(0).wait_send)
    pass_on(1)
    every.wait_recv()
    acc = mine
    for d in range(plane_n - 1):
        acc = acc + gp[d]
    ts[0] = acc
    dbl_wait(len(steps) - 1)
    order = sorted(range(1, line_n), key=lambda d: -min(d, line_n - d))
    for d in order:
        c = remote(ts.at[0], tr.at[d - 1], ls_sem, lr_sem, on_line(d))
        c.start()
    for i in range(6):
        wait_face(1, i)
    loads[10].wait()
    dev_old = strains(1, flats(1))
    jump = [[2.0 * shear_c[l] * (dev_new[l][a] - dev_old[l][a]) for a in range(6)] for l in range(2)]
    total = [[None] * 6 for _ in range(2)]
    for k in range(TERMS):
        for l in range(2):
            tau = pick([times[r, k] for r in range(REGIONS)], is_region[l])
            mod = pick([moduli[r, k] for r in range(REGIONS)], is_region[l])
            decay = jnp.exp(-1.0 / tau)
            weight = mod * (1.0 - decay) * tau
            for a in range(6):
                val = decay * visc[k, a, l] + weight * jump[l][a]
                vnext[k, a, l] = val
                total[l][a] = val if k == 0 else total[l][a] + val
    for l in range(2):
        sums = []
        for r in range(REGIONS):
            s = moduli[r, 0]
            for k in range(1, TERMS):
                s = s + moduli[r, k]
            sums.append(1.0 - s)
        factor = pick(sums, is_region[l]) * 2.0 * shear_c[l]
        for a in range(6):
            stress[a, l] = softening[l] * (factor * dev_new[l][a] + total[l][a])

    for group in (faces[1], edges):
        for c in group:
            c.wait_send()
    for cond, c in spread[:4]:
        pl.when(cond)(c.wait_send)
    pl.when(edge)(relay(1).wait_send)
    every.wait_send()
    along = remote(tr, tr, ls_sem, lr_sem, on_line(1))
    along.wait_recv()
    for d in range(line_n - 1):
        acc = acc + tr[d]
    sums_out[...] = acc
    along.wait_send()


def finish(stress, vnext, enext, vecs, sums, stress_h, vnext_h, enext_h, field_h, resid_h, field, resid, sem):
    stores = [pltpu.make_async_copy(a, b, sem.at[i]) for i, (a, b) in enumerate(
        ((vnext, vnext_h), (stress, stress_h), (enext, enext_h), (field, field_h), (resid, resid_h)))]
    for c in stores[:3]:
        c.start()
    full = jnp.broadcast_to(sums[...], (8, 128))
    gram = {pair: jnp.broadcast_to(full[:, n:n + 1], (8, 128)) for n, pair in enumerate(PAIRS)}
    on_field, on_resid = coefficients(gram)
    for l in range(2):
        val = on_field[0] * vecs[l]
        for k in range(1, ITERS):
            val = val + on_field[k] * vecs[2 * k + l]
        field[l] = val
        val = on_resid[0] * vecs[l]
        for k in range(1, ITERS + 1):
            val = val + on_resid[k] * vecs[2 * k + l]
        resid[l] = val
    for c in stores[3:]:
        c.start()
    for c in stores:
        c.wait()


def solution(mesh):
    nx, ny, nz = mesh.shape["gx"], mesh.shape["gy"], mesh.shape["gz"]
    zhi = 4 if nx % 32 == 0 else 2
    low_n = nx // zhi
    line_n, plane_n = zhi * nz, low_n * ny

    def on_device(*args):
        hbm = pl.BlockSpec(memory_space=pltpu.HBM)
        local = pl.BlockSpec(memory_space=pltpu.VMEM)
        vm = pltpu.VMEM
        sm = pltpu.SMEM
        dma = pltpu.SemaphoreType.DMA
        cells = jax.ShapeDtypeStruct((2, 8, 128), F32)
        stress = jax.ShapeDtypeStruct((6, 2, 8, 128), F32)
        visco = jax.ShapeDtypeStruct((6, 6, 2, 8, 128), F32)
        parts = pl.pallas_call(
            functools.partial(kernel, (nx, ny, nz, zhi)),
            out_shape=(stress, visco, cells,
                       jax.ShapeDtypeStruct((10, 8, 128), F32), jax.ShapeDtypeStruct((1, 128), F32)),
            in_specs=[hbm] * 11,
            out_specs=[local] * 5,
            scratch_shapes=[
                vm((3, 2, 8, 128), F32), vm((3, 2, 8, 128), F32), vm((6, 6, 2, 8, 128), F32),
                vm((2, 8, 128), F32), vm((2, 8, 128), jnp.int32), vm((2, 8, 128), jnp.int32),
                sm((4, 6), F32), sm((4, 6), F32), sm((4,), F32), sm((4,), F32), sm((4,), F32),
                vm((2, 2, 3, 8, 128), F32), vm((2, 3, 3, 8, 128), F32),
                vm((2, 2, 6, 1, 128), F32), vm((2, 2, 6, 1, 128), F32),
                vm((2, 2, 8, 128), F32), vm((2, 2, 8, 128), F32),
                vm((10, 8, 128), F32),
                vm((2, 8, 4, 128), F32), vm((2, 8, 4, 128), F32),
                vm((2, 8, 128), F32), vm((6, 8, 128), F32),
                vm((1, 1, 128), F32), vm((plane_n - 1, 1, 128), F32),
                vm((1, 1, 128), F32), vm((line_n - 1, 1, 128), F32),
                vm((11, 8, 128), F32), vm((17, 8, 128), F32), vm((3, 8, 128), F32),
                dma((6,)), dma((21,)), dma((31,)), dma, dma, dma, dma,
                pltpu.SemaphoreType.REGULAR((4,)),
            ],
            compiler_params=pltpu.CompilerParams(
                collective_id=0, has_side_effects=True, vmem_limit_bytes=16 << 20),
        )(*[pltpu.with_memory_space_constraint(a, pltpu.HBM) for a in args])
        return pl.pallas_call(
            finish,
            out_shape=(stress, visco, cells, cells, cells),
            in_specs=[local] * 5,
            out_specs=[hbm] * 5,
            scratch_shapes=[vm((2, 8, 128), F32), vm((2, 8, 128), F32), dma((5,))],
            compiler_params=pltpu.CompilerParams(vmem_limit_bytes=16 << 20),
        )(*parts)

    cell = P("gx", "gy", "gz")
    vec = P(None, "gx", "gy", "gz")
    ten = P(None, None, "gx", "gy", "gz")
    return jax.shard_map(
        on_device,
        mesh=mesh,
        in_specs=(vec, vec, ten, cell, cell, cell, P(), P(), P(), P(), P()),
        out_specs=(vec, ten, cell, cell, cell),
        check_vma=False,
    )
```

```python
import functools

import jax
import jax.numpy as jnp
from jax import lax
from jax.experimental import pallas as pl
from jax.experimental.pallas import tpu as pltpu
from jax.sharding import PartitionSpec as P

ITERS = 4
TERMS = 6
REGIONS = 4
SHIFTS = (1.0, 25.0, 25.0, 1.0)
PAIRS = tuple((i, j) for i in range(4) for j in range(i, 5))
F32 = jnp.float32


def flat_parts(grad_y, grad_z):
    return (grad_y[1], grad_z[2], 0.5 * (grad_z[1] + grad_y[2]), grad_z[0], grad_y[0])


def deviator(grad_x, flat):
    xx, yy, zz = grad_x[0], flat[0], flat[1]
    third = (xx + yy + zz) * (1.0 / 3.0)
    return (
        xx - third,
        yy - third,
        zz - third,
        flat[2],
        0.5 * (flat[3] + grad_x[2]),
        0.5 * (flat[4] + grad_x[1]),
    )


def coefficients(gram):
    def form(left, right):
        total = None
        for i, a in enumerate(left):
            row = None
            for j, b in enumerate(right):
                term = b * gram[(min(i, j), max(i, j))]
                row = term if row is None else row + term
            row = a * row
            total = row if total is None else total + row
        return total

    one = jnp.ones_like(gram[(0, 0)])
    res, direction, field = [one], [one], []
    norm = gram[(0, 0)]
    for step in range(ITERS):
        image = []
        for k in range(step + 2):
            value = None
            if k <= step:
                value = SHIFTS[k] * direction[k]
            if k >= 1:
                value = 24.0 * direction[k - 1] if value is None else value + 24.0 * direction[k - 1]
            image.append(value)
        alpha = norm / form(direction, image)
        field = [field[k] + alpha * direction[k] if k < step else alpha * direction[k] for k in range(step + 1)]
        res = [res[k] - alpha * image[k] if k <= step else -alpha * image[k] for k in range(step + 2)]
        if step + 1 < ITERS:
            new = form(res, res)
            beta = new / norm
            direction = [res[k] + beta * direction[k] if k <= step else res[k] for k in range(step + 2)]
            norm = new
    return field, res


def kernel(sizes, *refs):
    nx, ny, nz, zhi = sizes
    low_n = nx // zhi
    line_n = zhi * nz
    plane_n = low_n * ny
    half_way = nz // 2
    (disp_h, dold_h, visc_h, emax_h, reg_h, dir_h, moduli_h, times_h, shear_h, ratio_h, scale_h,
     stress, vnext, enext, vout, sums_out,
     disp, dold, visc, emax, reg, dirm, moduli, times, shear, ratio, scale,
     u, xr, ys, yr, zs, zr, e, eys, eyr, ezs, ezr, gs, gp, ts, tr,
     pk, mk, mu, ld_sem, ss, rs, ps_sem, pr_sem, ls_sem, lr_sem, dbl) = refs

    ix, iy, iz = lax.axis_index("gx"), lax.axis_index("gy"), lax.axis_index("gz")
    low, hi = lax.rem(ix, low_n), lax.div(ix, low_n)
    spot = hi * nz + iz
    place = low * ny + iy
    top = low == low_n - 1
    bottom = low == 0

    def wrap(q, n):
        return jnp.where(q >= n, q - n, q)

    def on_x(d):
        return {"gx": wrap(ix + d % nx, nx), "gy": iy, "gz": iz}

    def at(d, low_to, dy=0):
        q = wrap(spot + (d % line_n if isinstance(d, int) else d), line_n)
        y_to = wrap(iy + dy % ny, ny) if dy else iy
        return {"gx": lax.div(q, nz) * low_n + low_to, "gy": y_to, "gz": lax.rem(q, nz)}

    def on_line(d, dy=0):
        return at(d, low, dy)

    def on_plane(d):
        q = wrap(place + d, plane_n)
        return {"gx": hi * low_n + lax.div(q, ny), "gy": lax.rem(q, ny), "gz": iz}

    def either(cond, one, other):
        return {k: jnp.where(cond, one[k], other[k]) for k in one}

    def signal(sem, dev):
        pl.semaphore_signal(sem, inc=1, device_id=dev, device_id_type=pl.DeviceIdType.MESH)

    def remote(src, dst, ssem, rsem, dev):
        return pltpu.make_async_remote_copy(
            src_ref=src, dst_ref=dst, send_sem=ssem, recv_sem=rsem,
            device_id=dev, device_id_type=pl.DeviceIdType.MESH)

    loads = [pltpu.make_async_copy(a, b, ld_sem.at[i]) for i, a, b in (
        (0, dir_h, dirm), (1, disp_h, disp), (4, dold_h, dold), (2, reg_h, reg), (3, emax_h, emax),
        (0, shear_h, shear), (1, ratio_h, ratio), (2, scale_h, scale), (3, moduli_h, moduli), (5, times_h, times),
        (4, visc_h, visc))]
    for c in loads[:5]:
        c.start()

    barrier = pltpu.get_barrier_semaphore()
    greet = [at(s, wrap(low + r % low_n, low_n)) for r in (0, 1, -1, 2, -2) for s in (half_way, -half_way)]
    greet += [on_plane(d) for d in range(1, plane_n)]
    greet += [on_line(1), on_line(-1)]
    for dev in greet:
        signal(barrier, dev)

    row = lax.broadcasted_iota(jnp.int32, (8, 128), 0)
    lane = lax.broadcasted_iota(jnp.int32, (8, 128), 1)
    ylo_on = jnp.where(iy > 0, 1.0, 0.0).astype(F32)
    yhi_on = jnp.where(iy < ny - 1, 1.0, 0.0).astype(F32)
    zlo_on = jnp.where(iz > 0, 1.0, 0.0).astype(F32)
    zhi_on = jnp.where(iz < nz - 1, 1.0, 0.0).astype(F32)

    def hold(half, src):
        to_hi, to_lo = zero, zero
        for l in range(2):
            free = (1 - dirm[l]).astype(F32)
            for c in range(3):
                j = l * 3 + c
                val = src[c, l] * free
                u[half, l, c] = val
                ys[half, 0, j] = val[7:8]
                ys[half, 1, j] = val[0:1]
                to_hi = jnp.where(lane == j, pltpu.roll(val, (j - 127) % 128, 1), to_hi)
                to_lo = jnp.where(lane == j, pltpu.roll(val, j, 1) if j else val, to_lo)
        zs[half, 0] = to_hi
        zs[half, 1] = to_lo

    def send_faces(half):
        out = [
            remote(u.at[half, 1], xr.at[half, jnp.where(top, 2, 0)], ss.at[0],
                   rs.at[7 * half + jnp.where(top, 6, 0)], either(top, on_line(half_way), on_x(1))),
            remote(u.at[half, 0], xr.at[half, jnp.where(bottom, 2, 1)], ss.at[1],
                   rs.at[7 * half + jnp.where(bottom, 6, 1)], either(bottom, on_line(-half_way), on_x(-1))),
            remote(ys.at[half, 0], yr.at[half, 0], ss.at[2], rs.at[7 * half + 2], on_line(0, 1)),
            remote(ys.at[half, 1], yr.at[half, 1], ss.at[3], rs.at[7 * half + 3], on_line(0, -1)),
            remote(zs.at[half, 0], zr.at[half, 0], ss.at[4], rs.at[7 * half + 4], on_line(1)),
            remote(zs.at[half, 1], zr.at[half, 1], ss.at[5], rs.at[7 * half + 5], on_line(-1)),
        ]
        for c in out:
            c.start()
        return out

    def relay(half):
        side = jnp.where(top, 0, 1)
        return remote(xr.at[half, 2], xr.at[half, side], ss.at[6], rs.at[7 * half + side],
                      either(top, at(half_way, 0), at(-half_way, low_n - 1)))

    def pass_on(half):
        @pl.when(top | bottom)
        def _():
            remote(xr.at[half, 2], xr.at[half, 2], ss.at[6], rs.at[7 * half + 6], on_line(1)).wait_recv()
            relay(half).start()

    def wait_face(half, i):
        dst = (xr.at[half, 0], xr.at[half, 1], yr.at[half, 0], yr.at[half, 1], zr.at[half, 0], zr.at[half, 1])[i]
        remote(dst, dst, ss.at[i], rs.at[7 * half + i], on_line(1)).wait_recv()

    edge = top | bottom
    side = jnp.where(top, half_way, line_n - half_way)
    to_relay = on_line(side)
    telling = [
        remote(pk.at[pl.ds(0, 5)], mk.at[pl.ds(3, 5)], ss.at[11 + 0], rs.at[26 + 0], to_relay),
        remote(pk.at[pl.ds(5, 5)], mk.at[pl.ds(8, 5)], ss.at[11 + 1], rs.at[26 + 1], to_relay),
        remote(u.at[0, jnp.where(top, 1, 0)], mu, ss.at[11 + 2], rs.at[26 + 2],
               at(side, jnp.where(top, 0, low_n - 1))),
        remote(pk.at[pl.ds(10, 1)], mk.at[pl.ds(13, 1)], ss.at[11 + 3], rs.at[26 + 3], to_relay),
    ]
    first = at(side, jnp.where(top, 0, low_n - 1))
    second = at(side, jnp.where(top, 1, low_n - 2))
    slot_first, slot_second = jnp.where(top, 0, 1), jnp.where(top, 2, 3)

    def pass_layer(k, frm, count, to, sem, dev):
        return remote(mk.at[pl.ds(frm, count)], e.at[pl.ds(to, count)], ss.at[16 + k], rs.at[14 + sem], dev)

    passing = [
        pass_layer(0, 16, 1, jnp.where(top, 3, 6), slot_first, first),
        pass_layer(1, 16, 1, jnp.where(top, 1, 8), slot_second, second),
        pass_layer(2, 13, 1, jnp.where(top, 2, 7), slot_first, first),
        pass_layer(3, 13, 1, jnp.where(top, 0, 9), slot_second, second),
        pass_layer(4, 14, 2, jnp.where(top, 0, 8), slot_second, first),
    ]

    zero = jnp.zeros((8, 128), F32)
    loads[0].wait()
    loads[1].wait()
    hold(0, disp)
    loads[3].wait()
    loads[4].wait()
    for c in range(3):
        pk[c] = jnp.where(top, u[0, 0, c], u[0, 1, c])
    pk[3] = jnp.where(top, emax[1], emax[0])
    pk[4] = jnp.where(top, reg[1], reg[0]).astype(F32)
    pl.semaphore_wait(barrier, len(greet))
    faces = [send_faces(0)]

    @pl.when(edge)
    def _():
        telling[2].start()
        telling[0].start()

    for c in loads[5:10]:
        c.start()

    steps = []
    reach = 1
    while reach < line_n // 2:
        steps.append(reach)
        reach *= 2

    def dbl_signal(s):
        if s < len(steps):
            signal(dbl.at[s], on_line(steps[s]))
            signal(dbl.at[s], on_line(-steps[s]))

    known = set()

    def dbl_wait(s):
        if s < len(steps) and s not in known:
            known.add(s)
            pl.semaphore_wait(dbl.at[s], 2)

    dbl_signal(0)
    loads[2].wait()
    hold(1, dold)
    loads[10].start()
    for c in loads[5:10]:
        c.wait()
    dbl_wait(0)
    dbl_signal(1)

    def pick(table, where_is):
        out = table[REGIONS - 1]
        for k in range(REGIONS - 2, -1, -1):
            out = jnp.where(where_is[k], table[k], out)
        return out

    is_region = [[reg[l] == k for k in range(REGIONS)] for l in range(2)]
    shear_c = [pick([shear[k] for k in range(REGIONS)], is_region[l]) for l in range(2)]
    ratio_c = [pick([ratio[k] for k in range(REGIONS)], is_region[l]) for l in range(2)]
    scale_c = [pick([scale[k] for k in range(REGIONS)], is_region[l]) for l in range(2)]

    def flats(half):
        from_lo = zr[half, 0] * zlo_on
        from_hi = zr[half, 1] * zhi_on
        out = []
        for l in range(2):
            grad_y, grad_z = [], []
            for c in range(3):
                j = l * 3 + c
                val = u[half, l, c]
                below = jnp.broadcast_to(yr[half, 0, j] * ylo_on, (8, 128))
                above = jnp.broadcast_to(yr[half, 1, j] * yhi_on, (8, 128))
                prev_y = pltpu.roll(jnp.where(row == 7, below, val), 1, 0)
                next_y = pltpu.roll(jnp.where(row == 0, above, val), 7, 0)
                prev_z = jnp.where(lane == 0, pltpu.roll(from_lo, (128 - j) % 128, 1), pltpu.roll(val, 1, 1))
                next_z = jnp.where(lane == 127, pltpu.roll(from_hi, 127 - j, 1), pltpu.roll(val, 127, 1))
                grad_y.append(0.5 * (next_y - prev_y))
                grad_z.append(0.5 * (next_z - prev_z))
            out.append(flat_parts(grad_y, grad_z))
        return out

    def strains(half, flat):
        out = []
        for l in range(2):
            grad_x = []
            for c in range(3):
                prev_x = xr[half, 0, c] if l == 0 else u[half, 0, c]
                next_x = xr[half, 1, c] if l == 1 else u[half, 1, c]
                grad_x.append(0.5 * (next_x - prev_x))
            out.append(deviator(grad_x, flat[l]))
        return out

    def drive_of(d, g, r, m, most):
        energy = g * (
            d[0] * d[0] + d[1] * d[1] + d[2] * d[2] + 2.0 * (d[3] * d[3] + d[4] * d[4] + d[5] * d[5]))
        peak = jnp.maximum(most, energy)
        soft = 1.0 - lax.erf((peak - energy) / m) / r
        return peak, soft, soft * energy

    for i in range(2, 6):
        wait_face(0, i)
    flat_new = flats(0)
    for i in range(5):
        pk[5 + i] = jnp.where(top, flat_new[1][i], flat_new[0][i])

    @pl.when(edge)
    def _():
        telling[1].start()

    @pl.when(jnp.logical_not(bottom))
    def _():
        wait_face(0, 0)

    @pl.when(jnp.logical_not(top))
    def _():
        wait_face(0, 1)

    @pl.when(edge)
    def _():
        near = [xr[0, jnp.where(top, 0, 1), c] for c in range(3)]
        grad_x = [0.5 * (jnp.where(top, u[0, 1, c], near[c]) - jnp.where(top, near[c], u[0, 0, c]))
                  for c in range(3)]
        flat = [jnp.where(top, flat_new[0][i], flat_new[1][i]) for i in range(5)]
        both = [jnp.where(top, a, b) for a, b in (
            (shear_c[0], shear_c[1]), (ratio_c[0], ratio_c[1]), (scale_c[0], scale_c[1]), (emax[0], emax[1]))]
        pk[10] = drive_of(deviator(grad_x, flat), *both)[2]
        telling[3].start()

    dbl_wait(1)
    dbl_signal(2)
    pass_on(0)

    @pl.when(edge)
    def _():
        for c in telling[:3]:
            c.wait_recv()
        grad_x = [0.5 * (jnp.where(top, mu[c], mk[3 + c]) - jnp.where(top, mk[3 + c], mu[c])) for c in range(3)]
        theirs = [mk[7] == float(k) for k in range(REGIONS)]
        both = [pick([t[k] for k in range(REGIONS)], theirs) for t in (shear, ratio, scale)]
        mk[16] = drive_of(deviator(grad_x, [mk[8 + i] for i in range(5)]), *both, mk[6])[2]
        passing[0].start()
        passing[1].start()
        telling[3].wait_recv()
        passing[2].start()
        passing[3].start()
        remote(mk.at[pl.ds(14, 2)], mk.at[pl.ds(14, 2)], ss.at[11 + 4], rs.at[26 + 4], to_relay).wait_recv()
        passing[4].start()

    @pl.when(bottom)
    def _():
        wait_face(0, 0)

    @pl.when(top)
    def _():
        wait_face(0, 1)

    dev_new = strains(0, flat_new)
    softening = []
    for l in range(2):
        enext[l], soft, e[4 + l] = drive_of(dev_new[l], shear_c[l], ratio_c[l], scale_c[l], emax[l])
        softening.append(soft)

    own = e.at[pl.ds(4, 2)]
    wide = [
        remote(own, e.at[pl.ds(2, 2)], ss.at[7 + 0], rs.at[14 + 0], on_x(1)),
        remote(own, e.at[pl.ds(6, 2)], ss.at[7 + 1], rs.at[14 + 1], on_x(-1)),
        remote(own, e.at[pl.ds(0, 2)], ss.at[7 + 2], rs.at[14 + 2], on_x(2)),
        remote(own, e.at[pl.ds(8, 2)], ss.at[7 + 3], rs.at[14 + 3], on_x(-2)),
    ]
    under, above_ = low == low_n - 2, low == 1
    spread = list(zip((jnp.logical_not(top), jnp.logical_not(bottom), low < low_n - 2, low > 1), wide))
    spread.append((under | above_, remote(
        own, mk.at[pl.ds(14, 2)], ss.at[11 + 4], rs.at[26 + 4],
        at(jnp.where(under, half_way, line_n - half_way), jnp.where(under, low_n - 1, 0)))))
    for cond, c in reversed(spread):
        pl.when(cond)(c.start)
    for c in faces[0]:
        c.wait_send()
    faces.append(send_faces(1))
    dbl_wait(2)
    dbl_signal(3)

    row_mask = jnp.where(row < 4, yhi_on, ylo_on)
    lane_mask = jnp.where(lane < 4, zhi_on, jnp.where(lane >= 124, zlo_on, 0.0))
    masks = {(1, 0): row_mask, (0, 1): lane_mask, (1, 1): row_mask * lane_mask}
    to_hi, to_lo = zero, zero
    basis = {}
    for l in (4, 5, 2, 3, 6, 7, 0, 1, 8, 9):
        if l in (2, 6, 0, 8):
            wide[(2, 6, 0, 8).index(l)].wait_recv()
        val = e[l]
        basis[(l, 0, 0)] = val
        if 1 <= l <= 8:
            j = l - 1
            eys[0, j] = val[4:8]
            eys[1, j] = val[0:4]
            here = (lane >= 4 * j) & (lane < 4 * j + 4)
            to_hi = jnp.where(here, pltpu.roll(val, (4 * j - 124) % 128, 1), to_hi)
            to_lo = jnp.where(here, pltpu.roll(val, 4 * j, 1) if j else val, to_lo)
    ezs[0] = to_hi
    ezs[1] = to_lo
    edges = [
        remote(ezs.at[0], ezr.at[2], ss.at[11 + 0], rs.at[18 + 0], on_line(1, 1)),
        remote(ezs.at[0], ezr.at[3], ss.at[11 + 1], rs.at[18 + 1], on_line(1, -1)),
        remote(ezs.at[1], ezr.at[4], ss.at[11 + 2], rs.at[18 + 2], on_line(-1, 1)),
        remote(ezs.at[1], ezr.at[5], ss.at[11 + 3], rs.at[18 + 3], on_line(-1, -1)),
        remote(ezs.at[0], ezr.at[0], ss.at[11 + 4], rs.at[18 + 4], on_line(1)),
        remote(ezs.at[1], ezr.at[1], ss.at[11 + 5], rs.at[18 + 5], on_line(-1)),
        remote(eys.at[0], eyr.at[0], ss.at[11 + 6], rs.at[18 + 6], on_line(0, 1)),
        remote(eys.at[1], eyr.at[1], ss.at[11 + 7], rs.at[18 + 7], on_line(0, -1)),
    ]
    @pl.when(edge)
    def _():
        for c in telling + passing:
            c.wait_send()

    pl.when(under | above_)(spread[4][1].wait_send)
    for c in edges:
        c.start()
    for c in edges[6:]:
        c.wait_recv()
    for l in range(1, 9):
        basis[(l, 1, 0)] = jnp.concatenate([eyr[1, l - 1], eyr[0, l - 1]], axis=0) * row_mask
    for c in edges[:6]:
        c.wait_recv()
    sides = ((ezr[0], ezr[1]),
             (jnp.where(row < 4, ezr[3], ezr[2]), jnp.where(row < 4, ezr[5], ezr[4])))
    for l in range(1, 9):
        for t in range(2):
            j = l - 1
            from_lo, from_hi = sides[t]
            val = jnp.where(lane < 4,
                            pltpu.roll(from_hi, 128 - 4 * j, 1) if j else from_hi,
                            pltpu.roll(from_lo, 124 - 4 * j, 1))
            basis[(l, t, 1)] = val * masks[(t, 1)]

    def grow(now, k):
        cache = {}

        def rolled(key, amount, axis):
            at = (key, amount, axis)
            if at not in cache:
                cache[at] = pltpu.roll(now[key], amount, axis)
            return cache[at]

        out = {}
        for l in range(k + 1, 9 - k):
            inner = k + 2 <= l <= 7 - k
            for ty, tz in ((0, 0), (1, 0), (0, 1), (1, 1)) if inner else ((0, 0),):
                me = (l, ty, tz)
                acc = now[(l - 1, ty, tz)] + now[(l + 1, ty, tz)]
                acc = acc + jnp.where(row == 7, rolled((l, 1 - ty, tz), 7, 0), rolled(me, 7, 0))
                acc = acc + jnp.where(row == 0, rolled((l, 1 - ty, tz), 1, 0), rolled(me, 1, 0))
                acc = acc + jnp.where(lane == 127, rolled((l, ty, 1 - tz), 127, 1), rolled(me, 127, 1))
                acc = acc + jnp.where(lane == 0, rolled((l, ty, 1 - tz), 1, 1), rolled(me, 1, 1))
                acc = acc * (1.0 / 6.0)
                acc = now[me] - acc if SHIFTS[k] == 1.0 else -acc
                if (ty, tz) != (0, 0):
                    acc = acc * masks[(ty, tz)]
                out[me] = acc
        return out

    powers = [basis]
    for k in range(ITERS):
        powers.append(grow(powers[-1], k))
    vecs = [[p[(4, 0, 0)], p[(5, 0, 0)]] for p in powers]

    for k in range(ITERS + 1):
        for l in range(2):
            vout[2 * k + l] = vecs[k][l]
    sums = zero
    for n, (i, j) in enumerate(PAIRS):
        part = vecs[i][0] * vecs[j][0] + vecs[i][1] * vecs[j][1]
        sums = jnp.where(lane == n, jnp.sum(part, axis=1, keepdims=True), sums)
    mine = jnp.sum(sums, axis=0, keepdims=True)

    gs[0] = mine
    sends = []
    for d in sorted(range(1, plane_n), key=lambda d: -min(d, plane_n - d)):
        c = remote(gs.at[0], gp.at[d - 1], ps_sem, pr_sem, on_plane(d))
        c.start()
    every = remote(gp, gp, ps_sem, pr_sem, on_plane(1))
    pl.when(edge)(relay(0).wait_send)
    pass_on(1)
    every.wait_recv()
    acc = mine
    for d in range(plane_n - 1):
        acc = acc + gp[d]
    ts[0] = acc
    dbl_wait(len(steps) - 1)
    order = sorted(range(1, line_n), key=lambda d: -min(d, line_n - d))
    for d in order:
        c = remote(ts.at[0], tr.at[d - 1], ls_sem, lr_sem, on_line(d))
        c.start()
    for i in range(6):
        wait_face(1, i)
    loads[10].wait()
    dev_old = strains(1, flats(1))
    jump = [[2.0 * shear_c[l] * (dev_new[l][a] - dev_old[l][a]) for a in range(6)] for l in range(2)]
    total = [[None] * 6 for _ in range(2)]
    for k in range(TERMS):
        for l in range(2):
            tau = pick([times[r, k] for r in range(REGIONS)], is_region[l])
            mod = pick([moduli[r, k] for r in range(REGIONS)], is_region[l])
            decay = jnp.exp(-1.0 / tau)
            weight = mod * (1.0 - decay) * tau
            for a in range(6):
                val = decay * visc[k, a, l] + weight * jump[l][a]
                vnext[k, a, l] = val
                total[l][a] = val if k == 0 else total[l][a] + val
    for l in range(2):
        sums = []
        for r in range(REGIONS):
            s = moduli[r, 0]
            for k in range(1, TERMS):
                s = s + moduli[r, k]
            sums.append(1.0 - s)
        factor = pick(sums, is_region[l]) * 2.0 * shear_c[l]
        for a in range(6):
            stress[a, l] = softening[l] * (factor * dev_new[l][a] + total[l][a])

    for group in (faces[1], edges):
        for c in group:
            c.wait_send()
    for cond, c in spread[:4]:
        pl.when(cond)(c.wait_send)
    pl.when(edge)(relay(1).wait_send)
    every.wait_send()
    along = remote(tr, tr, ls_sem, lr_sem, on_line(1))
    along.wait_recv()
    for d in range(line_n - 1):
        acc = acc + tr[d]
    sums_out[...] = acc
    along.wait_send()


def finish(stress, vnext, enext, vecs, sums, stress_h, vnext_h, enext_h, field_h, resid_h, field, resid, sem):
    stores = [pltpu.make_async_copy(a, b, sem.at[i]) for i, (a, b) in enumerate(
        ((vnext, vnext_h), (stress, stress_h), (enext, enext_h), (field, field_h), (resid, resid_h)))]
    for c in stores[:3]:
        c.start()
    full = jnp.broadcast_to(sums[...], (8, 128))
    gram = {pair: jnp.broadcast_to(full[:, n:n + 1], (8, 128)) for n, pair in enumerate(PAIRS)}
    on_field, on_resid = coefficients(gram)
    for l in range(2):
        val = on_field[0] * vecs[l]
        for k in range(1, ITERS):
            val = val + on_field[k] * vecs[2 * k + l]
        field[l] = val
        val = on_resid[0] * vecs[l]
        for k in range(1, ITERS + 1):
            val = val + on_resid[k] * vecs[2 * k + l]
        resid[l] = val
    for c in stores[3:]:
        c.start()
    for c in stores:
        c.wait()


def solution(mesh):
    nx, ny, nz = mesh.shape["gx"], mesh.shape["gy"], mesh.shape["gz"]
    zhi = 4 if nx % 32 == 0 else 2
    low_n = nx // zhi
    line_n, plane_n = zhi * nz, low_n * ny

    def on_device(*args):
        hbm = pl.BlockSpec(memory_space=pltpu.HBM)
        local = pl.BlockSpec(memory_space=pltpu.VMEM)
        vm = pltpu.VMEM
        sm = pltpu.SMEM
        dma = pltpu.SemaphoreType.DMA
        cells = jax.ShapeDtypeStruct((2, 8, 128), F32)
        stress = jax.ShapeDtypeStruct((6, 2, 8, 128), F32)
        visco = jax.ShapeDtypeStruct((6, 6, 2, 8, 128), F32)
        parts = pl.pallas_call(
            functools.partial(kernel, (nx, ny, nz, zhi)),
            out_shape=(stress, visco, cells,
                       jax.ShapeDtypeStruct((10, 8, 128), F32), jax.ShapeDtypeStruct((1, 128), F32)),
            in_specs=[hbm] * 11,
            out_specs=[local] * 5,
            scratch_shapes=[
                vm((3, 2, 8, 128), F32), vm((3, 2, 8, 128), F32), vm((6, 6, 2, 8, 128), F32),
                vm((2, 8, 128), F32), vm((2, 8, 128), jnp.int32), vm((2, 8, 128), jnp.int32),
                sm((4, 6), F32), sm((4, 6), F32), sm((4,), F32), sm((4,), F32), sm((4,), F32),
                vm((2, 2, 3, 8, 128), F32), vm((2, 3, 3, 8, 128), F32),
                vm((2, 2, 6, 1, 128), F32), vm((2, 2, 6, 1, 128), F32),
                vm((2, 2, 8, 128), F32), vm((2, 2, 8, 128), F32),
                vm((10, 8, 128), F32),
                vm((2, 8, 4, 128), F32), vm((2, 8, 4, 128), F32),
                vm((2, 8, 128), F32), vm((6, 8, 128), F32),
                vm((1, 1, 128), F32), vm((plane_n - 1, 1, 128), F32),
                vm((1, 1, 128), F32), vm((line_n - 1, 1, 128), F32),
                vm((11, 8, 128), F32), vm((17, 8, 128), F32), vm((3, 8, 128), F32),
                dma((6,)), dma((21,)), dma((31,)), dma, dma, dma, dma,
                pltpu.SemaphoreType.REGULAR((4,)),
            ],
            compiler_params=pltpu.CompilerParams(
                collective_id=0, has_side_effects=True, vmem_limit_bytes=16 << 20),
        )(*[pltpu.with_memory_space_constraint(a, pltpu.HBM) for a in args])
        return pl.pallas_call(
            finish,
            out_shape=(stress, visco, cells, cells, cells),
            in_specs=[local] * 5,
            out_specs=[hbm] * 5,
            scratch_shapes=[vm((2, 8, 128), F32), vm((2, 8, 128), F32), dma((5,))],
            compiler_params=pltpu.CompilerParams(vmem_limit_bytes=16 << 20),
        )(*parts)

    cell = P("gx", "gy", "gz")
    vec = P(None, "gx", "gy", "gz")
    ten = P(None, None, "gx", "gy", "gz")
    return jax.shard_map(
        on_device,
        mesh=mesh,
        in_specs=(vec, vec, ten, cell, cell, cell, P(), P(), P(), P(), P()),
        out_specs=(vec, ten, cell, cell, cell),
        check_vma=False,
    )
```
